256 devices in a mesh: blk: 32 (over y, x, core), col: 8 (over z).
Axes of the slice: x: 4, y: 4, z: 8, core: 2. Of those that a mesh axis runs over, the one named last changes fastest.
Arguments:
- src_feat: bfloat16 [64, 1024, 256], P('blk', 'col'), may hold values from -40 to 40
- tgt_feat: bfloat16 [64, 1024, 256], P('blk', 'col'), may hold values from -40 to 40
- src_mass: bfloat16 [64, 1024], P('blk', 'col'), may hold values from 0.5 to 2
- tgt_mass: bfloat16 [64, 1024], P('blk', 'col'), may hold values from 0.5 to 2
- candidates: int32 [64, 8], P('blk'), may hold values from 0 to 63, as said below
- counts: int32 [64], P('blk'), may hold values from 1 to 8, as said below
- tgt_home: int32 [64], replicated, may hold values from 0 to 63, each once
Outputs:
- src_aligned: bfloat16 [64, 1024, 256], P('blk', 'col')
- tgt_aligned: bfloat16 [64, 1024, 256], P('blk', 'col')
The draws below stay inside these ranges and needn't reach their ends.
Inputs may be any that keep to these rules, and one draw needn't show every extreme that they name: `candidates`: each row's 8 entries are distinct; the first counts[i] of row i are live, the others are not used; every target block number is among the live entries of some row. `counts`: the 2 blocks of one index of blk hold at most 12 live slots together, and the blocks of some index hold exactly 12. A permutation: target block number j is stored as block tgt_home[j] of tgt_feat and tgt_mass.
All inputs are finite; a program needn't handle non-finite values.
Results may differ from the reference program's by a relative error of at most 0.017.
Values may be sent and summed in bfloat16 or wider, within the bound.
No kernel may reach another device: no remote copies, remote signals or barrier semaphores. Data moves between devices by JAX's collectives and lax.ppermute only.
A program may use at most 64 MiB of HBM per device.

```python
import math
import jax
import jax.numpy as jnp
from jax import lax

W = 256
B = 1024
KMAX = 8
ITERS = 2
BPD = 2
NB = 64


def feature_draw(key):
    key_one, key_two, key_three = jax.random.split(key, 3)
    row_scales = jnp.exp(jax.random.uniform(key_one, (NB, B, 1), jnp.float32, math.log(0.3), math.log(3.0)))
    col_scales = jnp.exp(jax.random.uniform(key_two, (1, 1, W), jnp.float32, math.log(0.3), math.log(3.0)))
    values = jax.random.normal(key_three, (NB, B, W), jnp.float32) * row_scales * col_scales
    return jnp.clip(values, -40.0, 40.0).astype(jnp.bfloat16)


def draw_src_feat(key, part):
    return feature_draw(jax.random.fold_in(key, 31))


def draw_tgt_feat(key, part):
    return feature_draw(jax.random.fold_in(key, 37))


def draw_candidates(key, part):
    key_one, key_two = jax.random.split(jax.random.fold_in(key, 11))
    leading = jax.random.permutation(key_one, NB).astype(jnp.int32)
    row_keys = jax.random.split(key_two, NB)
    offsets = jax.vmap(lambda row_key: jax.random.permutation(row_key, NB - 1)[:KMAX - 1] + 1)(row_keys)
    trailing = (leading[:, None] + offsets.astype(jnp.int32)) % NB
    return jnp.concatenate([leading[:, None], trailing], axis=1).astype(jnp.int32)


def draw_counts(key, part):
    key_one, key_two, key_three = jax.random.split(jax.random.fold_in(key, 23), 3)
    first_draw = jax.random.randint(key_one, (NB,), 0, 8)
    second_draw = jax.random.randint(key_two, (NB,), 0, 8)
    typical = 1 + first_draw * second_draw // 12
    loaded = jax.random.randint(key_three, (), 0, NB // BPD)
    position = jnp.arange(NB) % BPD
    forced = jnp.where(position == 0, KMAX, jnp.where(position == BPD - 1, 12 - KMAX, 6))
    in_group = jnp.arange(NB) // BPD == loaded
    return jnp.where(in_group, forced, typical).astype(jnp.int32)


def level_of(key, dims, cuts, smallest, high):
    factor_of = 1.0
    for axis_at, shards_of in cuts:
        heights = jax.random.uniform(jax.random.fold_in(jax.random.fold_in(key, 6), axis_at), (shards_of,), jnp.float32, smallest / len(cuts), high / len(cuts))
        factor_of = factor_of * jnp.repeat(jnp.exp(heights), dims[axis_at] // shards_of).reshape((-1,) + (1,) * (len(dims) - 1 - axis_at))
    return factor_of


def setup_inputs(seed: int = 0) -> dict:
    keys = jax.random.split(jax.random.key(seed), 8)
    src_feat = draw_src_feat(jax.random.fold_in(keys[7], 71), 0)
    tgt_feat = draw_tgt_feat(jax.random.fold_in(keys[7], 71), 0)
    src_mass = jnp.clip(jnp.exp(math.log(2.0) - 1.3862944 * jax.random.uniform(keys[2], (NB, B), jnp.float32) ** level_of(keys[2], (NB, B), ((0, 32), (1, 8)), -0.2, 0.2)), 0.5, 2.0).astype(jnp.bfloat16)
    tgt_mass = jnp.clip(jnp.exp(math.log(2.0) - 1.3862944 * jax.random.uniform(keys[3], (NB, B), jnp.float32) ** level_of(keys[3], (NB, B), ((0, 32), (1, 8)), -0.2, 0.2)), 0.5, 2.0).astype(jnp.bfloat16)
    candidates = draw_candidates(jax.random.fold_in(keys[7], 71), 0)
    counts = draw_counts(jax.random.fold_in(keys[7], 71), 0)
    tgt_home = jax.random.permutation(keys[6], NB).astype(jnp.int32)
    return dict(src_feat=src_feat, tgt_feat=tgt_feat, src_mass=src_mass, tgt_mass=tgt_mass, candidates=candidates, counts=counts, tgt_home=tgt_home)


score_offset = 0.3
softness_level = 0.02
epsilon = 1e-06
highest = lax.Precision.HIGHEST

def unit_rows(features):
    values = features.astype(jnp.float32)
    inverse = lax.rsqrt(lax.optimization_barrier(jnp.mean(values * values, axis=-1, keepdims=True)) + epsilon)
    return (values * inverse).astype(jnp.bfloat16)

def reference(src_feat, tgt_feat, src_mass, tgt_mass, candidates, counts, tgt_home):
    block_count, block_rows, feature_total = src_feat.shape
    slot_max = candidates.shape[1]
    src_unit = unit_rows(src_feat)
    tgt_unit = unit_rows(tgt_feat)
    src_weight = src_mass.astype(jnp.float32)
    tgt_weight = tgt_mass.astype(jnp.float32)
    slot_index = jnp.arange(block_count * slot_max, dtype=jnp.int32)
    src_of = (slot_index // slot_max).astype(jnp.int32)
    tgt_of = jnp.take(tgt_home, candidates.reshape(-1)).astype(jnp.int32)
    alive_flag = slot_index % slot_max < jnp.take(counts, src_of)
    slot_data = (src_of, tgt_of, alive_flag)

    def kernel_of(src_index, tgt_index):
        src_block = lax.dynamic_index_in_dim(src_unit, src_index, 0, keepdims=False)
        tgt_tile = lax.dynamic_index_in_dim(tgt_unit, tgt_index, 0, keepdims=False)
        score_matrix = jnp.dot(src_block, tgt_tile.T, preferred_element_type=jnp.float32)
        return jnp.exp((score_matrix / feature_total - score_offset) / softness_level)

    def row_pass(column_scaling_vector):

        def step(running, entry):
            src_index, tgt_index, alive = entry

            def compute_slot(current):
                kernel_tile = kernel_of(src_index, tgt_index)
                v_rows = lax.dynamic_index_in_dim(column_scaling_vector, tgt_index, 0, keepdims=False)
                row_part = jnp.dot(kernel_tile, v_rows, precision=highest)
                before = lax.dynamic_index_in_dim(current, src_index, 0, keepdims=False)
                return lax.dynamic_update_index_in_dim(current, before + row_part, src_index, 0)
            return (lax.cond(alive, compute_slot, lambda current: current, running), None)
        result, _ = lax.scan(step, jnp.zeros((block_count, block_rows), jnp.float32), slot_data)
        return result

    def col_pass(scaling_u):

        def step(running, entry):
            src_index, tgt_index, alive = entry

            def compute_slot(current):
                kernel_tile = kernel_of(src_index, tgt_index)
                u_rows = lax.dynamic_index_in_dim(scaling_u, src_index, 0, keepdims=False)
                col_part = jnp.dot(u_rows, kernel_tile, precision=highest)
                before = lax.dynamic_index_in_dim(current, tgt_index, 0, keepdims=False)
                return lax.dynamic_update_index_in_dim(current, before + col_part, tgt_index, 0)
            return (lax.cond(alive, compute_slot, lambda current: current, running), None)
        result, _ = lax.scan(step, jnp.zeros((block_count, block_rows), jnp.float32), slot_data)
        return result
    column_scaling_vector = jnp.ones((block_count, block_rows), jnp.float32)
    scaling_u = jnp.ones((block_count, block_rows), jnp.float32)
    for iteration in range(ITERS):
        scaling_u = src_weight / row_pass(column_scaling_vector)
        column_scaling_vector = tgt_weight / col_pass(scaling_u)

    def final_step(running, entry):
        src_index, tgt_index, alive = entry

        def compute_slot(current):
            src_sums, tgt_sums = current
            kernel_tile = kernel_of(src_index, tgt_index)
            u_rows = lax.dynamic_index_in_dim(scaling_u, src_index, 0, keepdims=False)
            v_rows = lax.dynamic_index_in_dim(column_scaling_vector, tgt_index, 0, keepdims=False)
            plan = (u_rows[:, None] * kernel_tile * v_rows[None, :]).astype(jnp.bfloat16)
            tgt_raw = lax.dynamic_index_in_dim(tgt_feat, tgt_index, 0, keepdims=False)
            src_raw = lax.dynamic_index_in_dim(src_feat, src_index, 0, keepdims=False)
            toward = jnp.dot(plan, tgt_raw, preferred_element_type=jnp.float32)
            back_terms = jnp.dot(plan.T, src_raw, preferred_element_type=jnp.float32)
            before_src = lax.dynamic_index_in_dim(src_sums, src_index, 0, keepdims=False)
            before_tgt = lax.dynamic_index_in_dim(tgt_sums, tgt_index, 0, keepdims=False)
            src_sums = lax.dynamic_update_index_in_dim(src_sums, before_src + toward, src_index, 0)
            tgt_sums = lax.dynamic_update_index_in_dim(tgt_sums, before_tgt + back_terms, tgt_index, 0)
            return (src_sums, tgt_sums)
        return (lax.cond(alive, compute_slot, lambda current: current, running), None)
    empty_sums = jnp.zeros((block_count, block_rows, feature_total), jnp.float32)
    (src_sums, tgt_sums), _ = lax.scan(final_step, (empty_sums, empty_sums), slot_data)
    src_aligned = (src_sums / src_weight[:, :, None]).astype(jnp.bfloat16)
    tgt_aligned = (tgt_sums / tgt_weight[:, :, None]).astype(jnp.bfloat16)
    return (src_aligned, tgt_aligned)
```

```python
import functools
import math

import jax
import jax.numpy as jnp
from jax import lax
from jax.experimental import pallas as pl
from jax.experimental.pallas import tpu as pltpu
from jax.sharding import PartitionSpec as P

PAIRS = 12
TEMP = 0.02
OFFSET = 0.3
EPS = 1e-06
F32 = jnp.float32
BF16 = jnp.bfloat16
SMEM = pl.BlockSpec(memory_space=pltpu.SMEM)
VMEM = pl.BlockSpec(memory_space=pltpu.VMEM)
ANY = pl.BlockSpec(memory_space=pl.ANY)
LIMIT = 28 * 1024 * 1024


def blk_perm(fn):
    pairs = []
    for i in range(32):
        y, x, k = fn(i // 8, (i // 2) % 4, i % 2)
        pairs.append((i, ((y % 4) * 4 + x % 4) * 2 + k))
    return pairs


def swap(v):
    return lax.ppermute(v, "blk", blk_perm(lambda y, x, k: (y, x, 1 - k)))


def from_x(v, d):
    return lax.ppermute(v, "blk", blk_perm(lambda y, x, k: (y, x - d, k)))


def from_y(v, d):
    return lax.ppermute(v, "blk", blk_perm(lambda y, x, k: (y - d, x, k)))


def from_first(v, d):
    return lax.ppermute(
        v, "blk", blk_perm(lambda y, x, k: (y, x - d, k) if k == 0 else (y - d, x, k))
    )


def from_second(v, d):
    return lax.ppermute(
        v, "blk", blk_perm(lambda y, x, k: (y - d, x, k) if k == 0 else (y, x - d, k))
    )


def from_z(v, d):
    return lax.ppermute(v, "col", [(i, (i - d) % 8) for i in range(8)])


def gather_targets(tgt_feat, core):
    mine = jnp.where(core == 0, tgt_feat[0], tgt_feat[1])
    other = jnp.where(core == 0, tgt_feat[1], tgt_feat[0])
    came = swap(other)
    pair = jnp.where(core == 0, jnp.stack([mine, came]), jnp.stack([came, mine]))
    near = jnp.concatenate([pair] + [from_first(pair, d) for d in (1, 2, 3)])
    parts = [near] + [from_second(near, d) for d in (1, 2, 3)]
    return parts + [swap(p) for p in parts]


def gather_sources(src_feat):
    left1, right1 = from_z(src_feat, -1), from_z(src_feat, 1)
    left2, right2 = from_z(left1, -1), from_z(right1, 1)
    left3, right3 = from_z(left2, -1), from_z(right2, 1)
    left4, right4 = from_z(left3[:1], -1), from_z(right3[1:], 1)
    return [src_feat, left1, left2, left3, right1, right2, right3, left4, right4]


CHUNK_OFFSETS = (0, -1, -2, -3, 1, 2, 3)


def col_sum_parts(v):
    left, right = from_z(v, -1), from_z(v, 1)
    three, two = v + left + right, v + left
    return three, from_z(three, 3), from_z(two, -2)


def blk_sum_parts(v):
    v = v + swap(v)
    v = v + sum(from_x(v, d) for d in (1, 3, 2))
    return (v,) + tuple(from_y(v, d) for d in (1, 3, 2))


def reduce_targets(mine, other, core):
    q = (mine.astype(F32) + swap(other).astype(F32)).astype(BF16).reshape(4, 8, 128, 256)
    s = q[0].astype(F32) + sum(from_first(q[d], 4 - d).astype(F32) for d in (1, 3, 2))
    s = s.astype(BF16).reshape(4, 2, 128, 256)
    t = s[0].astype(F32) + sum(from_second(s[d], 4 - d).astype(F32) for d in (1, 3, 2))
    keep = jnp.where(core == 0, t[0], t[1])
    came = swap(jnp.where(core == 0, t[1], t[0]).astype(BF16)).astype(F32)
    return jnp.where(core == 0, jnp.stack([keep, came]), jnp.stack([came, keep]))


def reduce_sources(parts):
    p = parts
    right, left = from_z(p[4, :1], -1), from_z(p[4, 1:], 1)
    a = jnp.stack([p[3, 0].astype(F32) + right[0].astype(F32), p[3, 1].astype(F32)]).astype(BF16)
    b = jnp.stack([p[5, 0].astype(F32), p[5, 1].astype(F32) + left[0].astype(F32)]).astype(BF16)
    right, left = from_z(a, -1), from_z(b, 1)
    for d in (2, 1):
        a = (p[d].astype(F32) + right.astype(F32)).astype(BF16)
        b = (p[8 - d].astype(F32) + left.astype(F32)).astype(BF16)
        right, left = from_z(a, -1), from_z(b, 1)
    return p[0].astype(F32) + right.astype(F32) + left.astype(F32)


def slot_of(meta, s):
    first = meta[2]
    p = jnp.where(s >= first, 1, 0)
    j = meta[20 + meta[4 + p * 8 + (s - first * p)]]
    return p, j


def live(meta):
    return meta[2] + meta[3]


def unit(rows):
    x = rows.astype(F32)
    return (x * lax.rsqrt(jnp.mean(x * x, axis=-1, keepdims=True) + EPS)).astype(BF16)


def two_rows(v):
    high = v.astype(BF16).astype(F32)
    row = lax.broadcasted_iota(jnp.int32, (16, v.shape[1]), 0)
    return jnp.where(row == 0, high, jnp.where(row == 1, v - high, 0.0)).astype(BF16)


def build_kernel(meta, *refs):
    src = refs[:9]
    tgt = refs[9:17]
    mass, kt, tiles, raw, rows, unit_src, acc, sems = refs[17:]
    n = live(meta)
    b, z = meta[0], meta[1]
    my_y, my_x, my_k = b // 8, (b // 2) % 4, b % 2

    def fetch(s, _):
        _, j = slot_of(meta, s)
        i, owner = j % 2, j // 2
        dy, dx = (owner // 8 - my_y) & 3, ((owner // 2) % 4 - my_x) & 3
        one, two = jnp.where(i == 0, dx, dy), jnp.where(i == 0, dy, dx)
        array = two + jnp.where(i == my_k, 0, 4)
        at = one * 2 + owner % 2
        for a in range(8):

            @pl.when(array == a)
            def _():
                pltpu.make_async_copy(tgt[a].at[at], tiles.at[s], sems.at[s]).start()

        return 0

    lax.fori_loop(0, n, fetch, 0)
    for c, d in enumerate(CHUNK_OFFSETS):
        at = pl.multiple_of(((z + d) & 7) * 128, 128)
        for p in range(2):
            chunk = src[c][p]
            raw[p, pl.ds(at, 128), :] = chunk
            unit_src[p, pl.ds(at, 128), :] = unit(chunk)
    at = pl.multiple_of(((z + 4) & 7) * 128, 128)
    for p in range(2):
        chunk = src[7 + p][0]
        raw[p, pl.ds(at, 128), :] = chunk
        unit_src[p, pl.ds(at, 128), :] = unit(chunk)
    acc[...] = jnp.zeros_like(acc)
    scale = math.log2(math.e) / (256 * TEMP)
    shift = OFFSET / TEMP * math.log2(math.e)

    def step(s, _):
        p, _j = slot_of(meta, s)
        pltpu.make_async_copy(tgt[0].at[0], tiles.at[s], sems.at[s]).wait()
        tile = unit(tiles[s])
        for c in range(4):
            cols = slice(c * 256, (c + 1) * 256)
            score = lax.dot_general(
                tile, unit_src[p, cols, :], (((1,), (1,)), ((), ())), preferred_element_type=F32
            )
            k = jnp.exp2(score * scale - shift)
            kt[s, :, cols] = k.astype(BF16)
            acc[p, :, cols] += k.reshape(16, 8, 256).sum(axis=0)
        return 0

    lax.fori_loop(0, n, step, 0)
    lane = lax.broadcasted_iota(jnp.int32, (1, 1024), 1) // 128
    for p in range(2):
        rows[p : p + 1, :] = jnp.sum(acc[p], axis=0, keepdims=True)
        own = jnp.concatenate([mass[p : p + 1, :].astype(F32)] * 8, axis=1)
        rows[2 + p : 3 + p, :] = jnp.where(lane == z, own, 0.0)


def col_kernel(first, meta, *refs):
    if first:
        kt, r0, r1, r2, tgt_mass, out, mass_out, u_rows = refs
        total = r0[...] + r1[...] + r2[...]
        mass = total[2:4]
        mass_out[...] = mass
    else:
        kt, r0, r1, r2, mass_in, out, u_out, u_rows = refs
        total = r0[...] + r1[...] + r2[...]
        mass = mass_in[...]
    u = mass / total[0:2]
    if not first:
        u_out[...] = u
    for p in range(2):
        u_rows[p] = two_rows(u[p : p + 1])
    out[...] = jnp.zeros_like(out)

    def step(s, _):
        p, j = slot_of(meta, s)
        part = lax.dot_general(
            u_rows[p], kt[s], (((1,), (1,)), ((), ())), preferred_element_type=F32
        )
        out[pl.ds(j, 1), :] += part[0:1] + part[1:2]
        return 0

    lax.fori_loop(0, live(meta), step, 0)
    if first:
        b = meta[0]
        out[pl.ds(64 + 2 * b, 1), :] = tgt_mass[0:1, :].astype(F32)
        out[pl.ds(65 + 2 * b, 1), :] = tgt_mass[1:2, :].astype(F32)


def row_kernel(meta, kt, c0, c1, c2, c3, out, mass_out, v_all, acc):
    total = (c0[...] + c1[...]) + (c2[...] + c3[...])
    mass_out[...] = total[64:]
    v_all[...] = total[64:] / total[:64]
    acc[...] = jnp.zeros_like(acc)

    def step(s, _):
        p, j = slot_of(meta, s)
        v = two_rows(v_all[pl.ds(j, 1), :])
        acc[p] += jnp.dot(v, kt[s], preferred_element_type=F32)[:8]
        return 0

    lax.fori_loop(0, live(meta), step, 0)
    for p in range(2):
        out[p : p + 1, :] = acc[p, 0:1, :] + acc[p, 1:2, :]


def back_kernel(meta, kt, u, raw, mine, other):
    b = meta[0]
    my_y, my_x, my_k = b // 8, (b // 2) % 4, b % 2
    mine[...] = jnp.zeros_like(mine)
    other[...] = jnp.zeros_like(other)

    def step(s, _):
        p, j = slot_of(meta, s)
        row = jnp.where(p == 0, u[0:1, :], u[1:2, :])
        plan = (kt[s].astype(F32) * row).astype(BF16)
        back = jnp.dot(plan, raw[p], preferred_element_type=F32)
        i, owner = j % 2, j // 2
        dy, dx = (owner // 8 - my_y) & 3, ((owner // 2) % 4 - my_x) & 3
        at = jnp.where(i == 0, dx * 8 + dy * 2, dy * 8 + dx * 2) + owner % 2

        @pl.when(i == my_k)
        def _():
            mine[at] = (mine[at].astype(F32) + back).astype(BF16)

        @pl.when(i != my_k)
        def _():
            other[at] = (other[at].astype(F32) + back).astype(BF16)

        return 0

    lax.fori_loop(0, live(meta), step, 0)


def toward_kernel(meta, kt, u, tiles, c0, c1, c2, c3, mass, out, v_out, v_all, acc):
    total = (c0[...] + c1[...]) + (c2[...] + c3[...])
    v_all[...] = mass[...] / total
    b, z = meta[0], meta[1]
    v_out[0:1, :] = v_all[pl.ds(2 * b, 1), :]
    v_out[1:2, :] = v_all[pl.ds(2 * b + 1, 1), :]
    acc[...] = jnp.zeros_like(acc)

    def step(s, _):
        p, j = slot_of(meta, s)
        v = jnp.broadcast_to(v_all[pl.ds(j, 1), :], (128, 128)).T
        row = jnp.where(p == 0, u[0:1, :], u[1:2, :])
        plan = []
        for c in range(8):
            cols = slice(c * 128, (c + 1) * 128)
            plan.append((kt[s, :, cols].astype(F32) * row[:, cols] * v).astype(BF16))
        plan = jnp.concatenate(plan, axis=1)
        acc[p] += lax.dot_general(
            plan, tiles[s], (((0,), (0,)), ((), ())), preferred_element_type=F32
        )
        return 0

    lax.fori_loop(0, live(meta), step, 0)
    for d in range(8):
        at = pl.multiple_of(((z + d) & 7) * 128, 128)
        for p in range(2):
            out[d, p] = acc[p, pl.ds(at, 128), :].astype(BF16)


def call(kernel, name, out_shape, in_specs, scratch, args, flops, nbytes):
    return pl.pallas_call(
        kernel,
        name=name,
        out_shape=out_shape,
        in_specs=in_specs,
        out_specs=[VMEM] * len(out_shape),
        scratch_shapes=scratch,
        compiler_params=pltpu.CompilerParams(vmem_limit_bytes=LIMIT),
        cost_estimate=pl.CostEstimate(flops=flops, bytes_accessed=nbytes, transcendentals=0),
    )(*args)


def local(src_feat, tgt_feat, src_mass, tgt_mass, candidates, counts, tgt_home):
    core = lax.axis_index("blk") % 2
    place = jnp.stack([lax.axis_index("blk"), lax.axis_index("col")]).astype(jnp.int32)
    meta = jnp.concatenate([place, counts, candidates.reshape(-1), tgt_home])
    sources = gather_sources(src_feat)
    targets = gather_targets(tgt_feat, core)
    S = jax.ShapeDtypeStruct
    kt, tiles, raw, rows = call(
        build_kernel,
        "build",
        [
            S((PAIRS, 128, 1024), BF16),
            S((PAIRS, 128, 256), BF16),
            S((2, 1024, 256), BF16),
            S((4, 1024), F32),
        ],
        [SMEM] + [VMEM] * 9 + [ANY] * 8 + [VMEM],
        [
            pltpu.VMEM((2, 1024, 256), BF16),
            pltpu.VMEM((2, 8, 1024), F32),
            pltpu.SemaphoreType.DMA((PAIRS,)),
        ],
        (meta, *sources, *targets, src_mass),
        800_000_000,
        7_000_000,
    )
    sums, mass_src = call(
        functools.partial(col_kernel, True),
        "col1",
        [S((128, 128), F32), S((2, 1024), F32)],
        [SMEM] + [VMEM] * 5,
        [pltpu.VMEM((2, 16, 1024), BF16)],
        (meta, kt, *col_sum_parts(rows), tgt_mass),
        100_000_000,
        3_000_000,
    )
    rows, mass_tgt = call(
        row_kernel,
        "row2",
        [S((2, 1024), F32), S((64, 128), F32)],
        [SMEM] + [VMEM] * 5,
        [pltpu.VMEM((64, 128), F32), pltpu.VMEM((2, 8, 1024), F32)],
        (meta, kt, *blk_sum_parts(sums)),
        100_000_000,
        3_000_000,
    )
    sums, u = call(
        functools.partial(col_kernel, False),
        "col2",
        [S((64, 128), F32), S((2, 1024), F32)],
        [SMEM] + [VMEM] * 5,
        [pltpu.VMEM((2, 16, 1024), BF16)],
        (meta, kt, *col_sum_parts(rows), mass_src),
        100_000_000,
        3_000_000,
    )
    mine, other = call(
        back_kernel,
        "back",
        [S((32, 128, 256), BF16)] * 2,
        [SMEM] + [VMEM] * 3,
        [],
        (meta, kt, u, raw),
        800_000_000,
        8_000_000,
    )
    parts = blk_sum_parts(sums)
    out, v = call(
        toward_kernel,
        "toward",
        [S((8, 2, 128, 256), BF16), S((2, 128), F32)],
        [SMEM] + [VMEM] * 8,
        [pltpu.VMEM((64, 128), F32), pltpu.VMEM((2, 1024, 256), F32)],
        (meta, kt, u, tiles, *parts, mass_tgt),
        800_000_000,
        6_000_000,
    )
    tgt_own = reduce_targets(mine, other, core)
    src_own = reduce_sources(out)
    src_aligned = (src_own / src_mass.astype(F32)[:, :, None]).astype(BF16)
    tgt_aligned = (tgt_own * v[:, :, None] / tgt_mass.astype(F32)[:, :, None]).astype(BF16)
    return (src_aligned, tgt_aligned)


def solution(mesh):
    in_specs = (
        P("blk", "col", None),
        P("blk", "col", None),
        P("blk", "col"),
        P("blk", "col"),
        P("blk", None),
        P("blk"),
        P(),
    )
    out_specs = (P("blk", "col", None), P("blk", "col", None))
    return jax.shard_map(local, mesh=mesh, in_specs=in_specs, out_specs=out_specs, check_vma=False)
```

```python
import functools
import math

import jax
import jax.numpy as jnp
from jax import lax
from jax.experimental import pallas as pl
from jax.experimental.pallas import tpu as pltpu
from jax.sharding import PartitionSpec as P


PAIRS = 12
TEMP = 0.02
OFFSET = 0.3
EPS = 1e-06
F32 = jnp.float32
BF16 = jnp.bfloat16
SMEM = pl.BlockSpec(memory_space=pltpu.SMEM)
VMEM = pl.BlockSpec(memory_space=pltpu.VMEM)
ANY = pl.BlockSpec(memory_space=pl.ANY)
LIMIT = 16 * 1024 * 1024


def blk_perm(fn):
    pairs = []
    for i in range(32):
        y, x, k = fn(i // 8, (i // 2) % 4, i % 2)
        pairs.append((i, (y * 4 + x) * 2 + k))
    return pairs


def swap(v):
    return lax.ppermute(v, "blk", blk_perm(lambda y, x, k: (y, x, 1 - k)))


def over_x(v, d):
    return lax.ppermute(v, "blk", blk_perm(lambda y, x, k: (y, x ^ d, k)))


def over_y(v, d):
    return lax.ppermute(v, "blk", blk_perm(lambda y, x, k: (y ^ d, x, k)))


def over_first(v, d):
    return lax.ppermute(
        v, "blk", blk_perm(lambda y, x, k: (y, x ^ d, k) if k == 0 else (y ^ d, x, k))
    )


def over_second(v, d):
    return lax.ppermute(
        v, "blk", blk_perm(lambda y, x, k: (y ^ d, x, k) if k == 0 else (y, x ^ d, k))
    )


def over_z(v, d):
    return lax.ppermute(v, "col", [(i, i ^ d) for i in range(8)])


def ring(v):
    pairs = []
    for i in range(256):
        z = i % 8
        pairs.append((i, i - z + (z + (1 if (i // 8) % 2 == 0 else -1)) % 8))
    return lax.ppermute(v, ("blk", "col"), pairs)


def pick(core, zero, one):
    return jnp.where(core == 0, zero, one)


def gather_targets(tgt_feat, core):
    came = swap(tgt_feat)
    pair = pick(core, jnp.stack([tgt_feat[0], came[0]]), jnp.stack([came[1], tgt_feat[1]]))
    near = jnp.concatenate([pair] + [over_first(pair, d) for d in (1, 2, 3)])
    parts = [near] + [over_second(near, d) for d in (1, 2, 3)]
    return parts + [swap(p) for p in parts]


def gather_sources(src_feat, core):
    came = swap(src_feat)
    chunk = pick(core, jnp.concatenate([src_feat, came]), jnp.concatenate([came, src_feat]))
    one = ring(chunk)
    two = ring(one)
    three = ring(two)
    four = ring(pick(core, three[:2], three[2:]))
    give = jnp.concatenate([pick(core, c[2:], c[:2]) for c in (one, two)])
    return [src_feat, one, two, three, four, swap(give), swap(pick(core, three[2:], three[:2]))]


def col_sum_parts(v):
    v = v + over_z(v, 1)
    return (v,) + tuple(over_z(v, d) for d in (2, 6, 4))


def blk_sum_parts(v):
    v = v + swap(v.astype(BF16)).astype(F32)
    low = v.astype(BF16)
    v = v + sum(over_x(low, d).astype(F32) for d in (1, 3, 2))
    low = v.astype(BF16)
    parts = [v]
    for d in (1, 3, 2):
        parts.append(over_y(low, d))
    return parts


def reduce_targets(mine, came, core):
    q = (mine.astype(F32) + came.astype(F32)).astype(BF16).reshape(4, 8, 128, 256)
    s = q[0].astype(F32)
    for d in (1, 3, 2):
        s = s + over_first(q[d], d).astype(F32)
    s = s.astype(BF16).reshape(4, 2, 128, 256)
    t = s[0].astype(F32) + sum(over_second(s[d], d).astype(F32) for d in (1, 3, 2))
    keep = pick(core, t[0], t[1])
    came = swap(pick(core, t[1], t[0]).astype(BF16)).astype(F32)
    return pick(core, jnp.stack([keep, came]), jnp.stack([came, keep]))


def reduce_sources(own, keep, give, far, core):
    got = swap(give)

    def add(m, d):
        k, g = keep[d - 1].astype(F32), got[d - 1].astype(F32)
        m = m.astype(F32)
        return (pick(core, jnp.concatenate([k, g]), jnp.concatenate([g, k])) + m).astype(BF16)

    last = ring(far)
    none = jnp.zeros_like(last)
    moving = pick(core, jnp.concatenate([last, none]), jnp.concatenate([none, last]))
    for d in (3, 2, 1):
        moving = ring(add(moving, d))
    came = swap(pick(core, moving[2:], moving[:2]))
    return own.astype(F32) + pick(core, moving[:2], moving[2:]).astype(F32) + came.astype(F32)


def slot_of(meta, s):
    counts, candidates, home = meta
    first = counts[0]
    p = jnp.where(s >= first, 1, 0)
    return p, home[candidates[p, s - first * p]]


def live(meta):
    return meta[0][0] + meta[0][1]


def place():
    b = lax.axis_index("blk")
    return b, lax.axis_index("col"), b // 8, (b // 2) % 4, b % 2


def unit(rows):
    x = rows.astype(F32)
    return (x * lax.rsqrt(jnp.mean(x * x, axis=-1, keepdims=True) + EPS)).astype(BF16)


def two_rows(v):
    high = v.astype(BF16).astype(F32)
    row = lax.broadcasted_iota(jnp.int32, (16, v.shape[1]), 0)
    return jnp.where(row == 0, high, jnp.where(row == 1, v - high, 0.0)).astype(BF16)


def build_kernel(*refs):
    meta, refs = refs[:3], refs[3:]
    own, one, two, three, four, far12, far3 = refs[:7]
    tgt = refs[7:15]
    mass, kt, tiles, raw, rows, unit_src, acc, sems, row_sems = refs[15:]
    n = live(meta)
    _, z, my_y, my_x, my_k = place()
    sign = 2 * my_k - 1
    chunks = []
    for p in range(2):
        chunks.append((own.at[p], z, p))
        for d, ref in ((1, one), (2, two), (3, three)):
            chunks.append((ref.at[2 * my_k + p], z + sign * d, p))
        chunks.append((four.at[p], z + 4, p))
        chunks.append((far12.at[p], z - sign, p))
        chunks.append((far12.at[2 + p], z - sign * 2, p))
        chunks.append((far3.at[p], z - sign * 3, p))
    copies = []
    for c, (ref, at, p) in enumerate(chunks):
        at = pl.multiple_of((at & 7) * 128, 128)
        copies.append((pltpu.make_async_copy(ref, raw.at[p, pl.ds(at, 128), :], row_sems.at[c]), at, p))
        copies[-1][0].start()

    def fetch(s, _):
        _, j = slot_of(meta, s)
        i, owner = j % 2, j // 2
        dy, dx = (owner // 8) ^ my_y, ((owner // 2) % 4) ^ my_x
        first, second = jnp.where(i == 0, dx, dy), jnp.where(i == 0, dy, dx)
        array = second + jnp.where(i == my_k, 0, 4)
        at = first * 2 + owner % 2
        for a in range(8):

            @pl.when(array == a)
            def _():
                pltpu.make_async_copy(tgt[a].at[at], tiles.at[s], sems.at[s]).start()

        return 0

    lax.fori_loop(0, n, fetch, 0)
    for copy, at, p in copies:
        copy.wait()
        unit_src[p, pl.ds(at, 128), :] = unit(raw[p, pl.ds(at, 128), :])
    acc[...] = jnp.zeros_like(acc)
    scale = math.log2(math.e) / (256 * TEMP)
    shift = OFFSET / TEMP * math.log2(math.e)

    def step(s, _):
        p, _ = slot_of(meta, s)
        pltpu.make_async_copy(tgt[0].at[0], tiles.at[s], sems.at[s]).wait()
        tile = unit(tiles[s])
        for c in range(4):
            cols = slice(c * 256, (c + 1) * 256)
            score = lax.dot_general(
                tile, unit_src[p, cols, :], (((1,), (1,)), ((), ())), preferred_element_type=F32
            )
            k = jnp.exp2(score * scale - shift)
            kt[s, :, cols] = k.astype(BF16)
            acc[p, :, cols] += k.reshape(16, 8, 256).sum(axis=0)
        return 0

    lax.fori_loop(0, n, step, 0)
    lane = lax.broadcasted_iota(jnp.int32, (1, 1024), 1) // 128
    for p in range(2):
        rows[p : p + 1, :] = jnp.sum(acc[p], axis=0, keepdims=True)
        own = jnp.concatenate([mass[p : p + 1, :].astype(F32)] * 8, axis=1)
        rows[2 + p : 3 + p, :] = jnp.where(lane == z, own, 0.0)


def col_kernel(first, *refs):
    meta, refs = refs[:3], refs[3:]
    if first:
        kt, r0, r1, r2, r3, tgt_mass, out, mass_out, u_rows = refs
        total = (r0[...] + r1[...]) + (r2[...] + r3[...])
        mass = total[2:4]
        mass_out[...] = mass
    else:
        kt, r0, r1, r2, r3, mass_in, out, u_out, u_rows = refs
        total = (r0[...] + r1[...]) + (r2[...] + r3[...])
        mass = mass_in[...]
    u = mass / total[0:2]
    if not first:
        u_out[...] = u
    for p in range(2):
        u_rows[p] = two_rows(u[p : p + 1])
    out[...] = jnp.zeros_like(out)

    def step(s, _):
        p, j = slot_of(meta, s)
        part = lax.dot_general(
            u_rows[p], kt[s], (((1,), (1,)), ((), ())), preferred_element_type=F32
        )
        out[pl.ds(j, 1), :] += part[0:1] + part[1:2]
        return 0

    lax.fori_loop(0, live(meta), step, 0)
    if first:
        b = place()[0]
        out[pl.ds(64 + 2 * b, 1), :] = tgt_mass[0:1, :].astype(F32)
        out[pl.ds(65 + 2 * b, 1), :] = tgt_mass[1:2, :].astype(F32)


def row_kernel(*refs):
    meta, refs = refs[:3], refs[3:]
    kt, c0, c1, c2, c3, out, mass_out, v_all, acc = refs
    total = c0[...] + c1[...].astype(F32) + c2[...].astype(F32) + c3[...].astype(F32)
    mass_out[...] = total[64:]
    v_all[...] = total[64:] / total[:64]
    acc[...] = jnp.zeros_like(acc)

    def step(s, _):
        p, j = slot_of(meta, s)
        v = two_rows(v_all[pl.ds(j, 1), :])
        acc[p] += jnp.dot(v, kt[s], preferred_element_type=F32)[:8]
        return 0

    lax.fori_loop(0, live(meta), step, 0)
    for p in range(2):
        out[p : p + 1, :] = acc[p, 0:1, :] + acc[p, 1:2, :]


def back_kernel(*refs):
    meta, refs = refs[:3], refs[3:]
    kt, u, raw, mine, other = refs
    _, _, my_y, my_x, my_k = place()
    mine[...] = jnp.zeros_like(mine)
    other[...] = jnp.zeros_like(other)

    def step(s, _):
        p, j = slot_of(meta, s)
        row = jnp.where(p == 0, u[0:1, :], u[1:2, :])
        plan = (kt[s].astype(F32) * row).astype(BF16)
        back = jnp.dot(plan, raw[p], preferred_element_type=F32)
        i, owner = j % 2, j // 2
        dy, dx = (owner // 8) ^ my_y, ((owner // 2) % 4) ^ my_x
        at = jnp.where(i == 0, dx * 8 + dy * 2, dy * 8 + dx * 2) + owner % 2

        @pl.when(i == my_k)
        def _():
            mine[at] = (mine[at].astype(F32) + back).astype(BF16)

        @pl.when(i != my_k)
        def _():
            other[at] = (other[at].astype(F32) + back).astype(BF16)

        return 0

    lax.fori_loop(0, live(meta), step, 0)


def toward_kernel(*refs):
    meta, refs = refs[:3], refs[3:]
    kt, u, tiles, c0, c1, c2, c3, mass, own, keep, give, far, v_out, v_all, acc = refs
    total = c0[...] + c1[...].astype(F32) + c2[...].astype(F32) + c3[...].astype(F32)
    v_all[...] = mass[...] / total
    b, z = place()[:2]
    v_out[0:1, :] = v_all[pl.ds(2 * b, 1), :]
    v_out[1:2, :] = v_all[pl.ds(2 * b + 1, 1), :]
    acc[...] = jnp.zeros_like(acc)

    def step(s, _):
        p, j = slot_of(meta, s)
        v = jnp.broadcast_to(v_all[pl.ds(j, 1), :], (128, 128)).T
        row = jnp.where(p == 0, u[0:1, :], u[1:2, :])
        plan = []
        for c in range(8):
            cols = slice(c * 128, (c + 1) * 128)
            plan.append((kt[s, :, cols].astype(F32) * row[:, cols] * v).astype(BF16))
        plan = jnp.concatenate(plan, axis=1)
        acc[p] += lax.dot_general(
            plan, tiles[s], (((0,), (0,)), ((), ())), preferred_element_type=F32
        )
        return 0

    lax.fori_loop(0, live(meta), step, 0)
    sign = 1 - 2 * (b % 2)
    for p in range(2):
        for ref, d in ((own, 0), (far, 4)):
            at = pl.multiple_of(((z + d) & 7) * 128, 128)
            ref[p] = acc[p, pl.ds(at, 128), :].astype(BF16)
        for ref, way in ((keep, sign), (give, -sign)):
            for d in (1, 2, 3):
                at = pl.multiple_of(((z + way * d) & 7) * 128, 128)
                ref[d - 1, p] = acc[p, pl.ds(at, 128), :].astype(BF16)


def call(kernel, out_shape, in_specs, scratch, args, flops, nbytes):
    return pl.pallas_call(
        kernel,
        out_shape=out_shape,
        in_specs=in_specs,
        out_specs=[VMEM] * len(out_shape),
        scratch_shapes=scratch,
        compiler_params=pltpu.CompilerParams(vmem_limit_bytes=LIMIT),
        cost_estimate=pl.CostEstimate(flops=flops, bytes_accessed=nbytes, transcendentals=0),
    )(*args)


def program(src_feat, tgt_feat, src_mass, tgt_mass, candidates, counts, tgt_home):
    core = lax.axis_index("blk") % 2
    meta = (counts, candidates, tgt_home)
    sources = gather_sources(src_feat, core)
    targets = gather_targets(tgt_feat, core)
    S = jax.ShapeDtypeStruct
    kt, tiles, raw, rows = call(
        build_kernel,
        [
            S((PAIRS, 128, 1024), BF16),
            S((PAIRS, 128, 256), BF16),
            S((2, 1024, 256), BF16),
            S((4, 1024), F32),
        ],
        [SMEM] * 3 + [ANY] * 15 + [VMEM],
        [
            pltpu.VMEM((2, 1024, 256), BF16),
            pltpu.VMEM((2, 8, 1024), F32),
            pltpu.SemaphoreType.DMA((PAIRS,)),
            pltpu.SemaphoreType.DMA((16,)),
        ],
        (*meta, *sources, *targets, src_mass),
        800_000_000,
        7_000_000,
    )
    sums, mass_src = call(
        functools.partial(col_kernel, True),
        [S((128, 128), F32), S((2, 1024), F32)],
        [SMEM] * 3 + [VMEM] * 6,
        [pltpu.VMEM((2, 16, 1024), BF16)],
        (*meta, kt, *col_sum_parts(rows), tgt_mass),
        100_000_000,
        3_000_000,
    )
    rows, mass_tgt = call(
        row_kernel,
        [S((2, 1024), F32), S((64, 128), F32)],
        [SMEM] * 3 + [VMEM] * 5,
        [pltpu.VMEM((64, 128), F32), pltpu.VMEM((2, 8, 1024), F32)],
        (*meta, kt, *blk_sum_parts(sums)),
        100_000_000,
        3_000_000,
    )
    sums, u = call(
        functools.partial(col_kernel, False),
        [S((64, 128), F32), S((2, 1024), F32)],
        [SMEM] * 3 + [VMEM] * 6,
        [pltpu.VMEM((2, 16, 1024), BF16)],
        (*meta, kt, *col_sum_parts(rows), mass_src),
        100_000_000,
        3_000_000,
    )
    mine, other = call(
        back_kernel,
        [S((32, 128, 256), BF16)] * 2,
        [SMEM] * 3 + [VMEM] * 3,
        [],
        (*meta, kt, u, raw),
        800_000_000,
        8_000_000,
    )
    came = swap(other)
    parts = blk_sum_parts(sums)
    tgt_own = reduce_targets(mine, came, core)
    own, keep, give, far, v = call(
        toward_kernel,
        [S((2, 128, 256), BF16)]
        + [S((3, 2, 128, 256), BF16)] * 2
        + [S((2, 128, 256), BF16), S((2, 128), F32)],
        [SMEM] * 3 + [VMEM] * 8,
        [pltpu.VMEM((64, 128), F32), pltpu.VMEM((2, 1024, 256), F32)],
        (*meta, kt, u, tiles, *parts, mass_tgt),
        800_000_000,
        6_000_000,
    )
    src_own = reduce_sources(own, keep, give, far, core)
    src_aligned = (src_own / src_mass.astype(F32)[:, :, None]).astype(BF16)
    tgt_aligned = (tgt_own * v[:, :, None] / tgt_mass.astype(F32)[:, :, None]).astype(BF16)
    return (src_aligned, tgt_aligned)


def solution(mesh):
    in_specs = (
        P("blk", "col", None),
        P("blk", "col", None),
        P("blk", "col"),
        P("blk", "col"),
        P("blk", None),
        P("blk"),
        P(),
    )
    out_specs = (P("blk", "col", None), P("blk", "col", None))
    return jax.shard_map(program, mesh=mesh, in_specs=in_specs, out_specs=out_specs, check_vma=False)
```

```python
import functools
import math

import jax
import jax.numpy as jnp
from jax import lax
from jax.experimental import pallas as pl
from jax.experimental.pallas import tpu as pltpu
from jax.sharding import PartitionSpec as P


PAIRS = 12
TEMP = 0.02
OFFSET = 0.3
EPS = 1e-06
F32 = jnp.float32
BF16 = jnp.bfloat16
SMEM = pl.BlockSpec(memory_space=pltpu.SMEM)
VMEM = pl.BlockSpec(memory_space=pltpu.VMEM)
ANY = pl.BlockSpec(memory_space=pl.ANY)
LIMIT = 16 * 1024 * 1024


def blk_perm(fn):
    pairs = []
    for i in range(32):
        y, x, k = fn(i // 8, (i // 2) % 4, i % 2)
        pairs.append((i, (y * 4 + x) * 2 + k))
    return pairs


def swap(v):
    return lax.ppermute(v, "blk", blk_perm(lambda y, x, k: (y, x, 1 - k)))


def over_x(v, d):
    return lax.ppermute(v, "blk", blk_perm(lambda y, x, k: (y, x ^ d, k)))


def over_y(v, d):
    return lax.ppermute(v, "blk", blk_perm(lambda y, x, k: (y ^ d, x, k)))


def over_first(v, d):
    return lax.ppermute(
        v, "blk", blk_perm(lambda y, x, k: (y, x ^ d, k) if k == 0 else (y ^ d, x, k))
    )


def over_second(v, d):
    return lax.ppermute(
        v, "blk", blk_perm(lambda y, x, k: (y ^ d, x, k) if k == 0 else (y, x ^ d, k))
    )


def over_z(v, d):
    return lax.ppermute(v, "col", [(i, i ^ d) for i in range(8)])


def along_z(v, odd):
    pairs = []
    for i in range(256):
        z, core = i % 8, (i // 8) % 2
        pairs.append((i, i - z + (((z + core + odd) ^ 1) - core - odd) % 8))
    return lax.ppermute(v, ("blk", "col"), pairs)


def pick(core, zero, one):
    return jnp.where(core == 0, zero, one)


def gather_targets(tgt_feat, core):
    came = swap(tgt_feat)
    pair = pick(core, jnp.stack([tgt_feat[0], came[0]]), jnp.stack([came[1], tgt_feat[1]]))
    near = [pair]
    for d in (1, 2, 3):
        near.append(over_first(pair, d))
    near = jnp.concatenate(near)
    parts = [near]
    for d in (1, 2, 3):
        parts.append(over_second(near, d))
    for n in range(4):
        parts.append(swap(parts[n]))
    return parts


def gather_sources(src_feat, even):
    came = along_z(src_feat, 0)
    pairs = [jnp.where(even, jnp.stack([src_feat, came]), jnp.stack([came, src_feat]))]
    for step in (2, 3, 4):
        pairs.append(along_z(pairs[-1], (step + 1) % 2))
    return pairs


def col_sum_parts(v):
    v = v + over_z(v, 1)
    return (v,) + tuple(over_z(v, d) for d in (5, 2, 6))


def blk_sum_parts(v):
    v = v + swap(v.astype(BF16)).astype(F32)
    low = v.astype(BF16)
    v = v + sum(over_x(low, d).astype(F32) for d in (1, 3, 2))
    low = v.astype(BF16)
    parts = [v]
    for d in (1, 3, 2):
        parts.append(over_y(low, d))
    return parts


def reduce_targets(mine, came, core):
    q = (mine.astype(F32) + came.astype(F32)).astype(BF16).reshape(4, 8, 128, 256)
    s = q[0].astype(F32)
    for d in (1, 3, 2):
        s = s + over_first(q[d], d).astype(F32)
    s = s.astype(BF16).reshape(4, 2, 128, 256)
    t = s[0].astype(F32)
    for d in (1, 3, 2):
        t = t + over_second(s[d], d).astype(F32)
    keep = pick(core, t[0], t[1])
    came = swap(pick(core, t[1], t[0]).astype(BF16)).astype(F32)
    return pick(core, jnp.stack([keep, came]), jnp.stack([came, keep]))


def reduce_sources(parts, even):
    moving = along_z(parts[3], 1)
    for step in (2, 1):
        moving = along_z((parts[step].astype(F32) + moving.astype(F32)).astype(BF16), step % 2)
    pair = parts[0].astype(F32) + moving.astype(F32)
    came = along_z(jnp.where(even, pair[1], pair[0]).astype(BF16), 0)
    return jnp.where(even, pair[0], pair[1]) + came.astype(F32)


def slot_of(meta, s):
    counts, candidates, home = meta
    first = counts[0]
    p = jnp.where(s >= first, 1, 0)
    return p, home[candidates[p, s - first * p]]


def live(meta):
    return meta[0][0] + meta[0][1]


def place():
    b = lax.axis_index("blk")
    return b, lax.axis_index("col"), b // 8, (b // 2) % 4, b % 2


def chunk_places(b, z):
    core = b % 2
    half = (z + core) & 7
    way = 1 - 2 * (half % 2)
    places = []
    for off in (0, -way, way, 2):
        first = 2 * (half // 2 + off)
        places.append([pl.multiple_of(((first + h - core) & 7) * 128, 128) for h in range(2)])
    return places


def unit(rows):
    x = rows.astype(F32)
    return (x * lax.rsqrt(jnp.mean(x * x, axis=-1, keepdims=True) + EPS)).astype(BF16)


def two_rows(v):
    high = v.astype(BF16).astype(F32)
    row = lax.broadcasted_iota(jnp.int32, (16, v.shape[1]), 0)
    return jnp.where(row == 0, high, jnp.where(row == 1, v - high, 0.0)).astype(BF16)


def build_kernel(*refs):
    meta, refs = refs[:3], refs[3:]
    src = refs[:4]
    tgt = refs[4:12]
    mass, kt, tiles, raw, rows, unit_src, acc, sems = refs[12:]
    n = live(meta)
    b, z, my_y, my_x, my_k = place()

    def fetch(s, _):
        _, j = slot_of(meta, s)
        i, owner = j % 2, j // 2
        dy, dx = (owner // 8) ^ my_y, ((owner // 2) % 4) ^ my_x
        first, second = jnp.where(i == 0, dx, dy), jnp.where(i == 0, dy, dx)
        array = second + jnp.where(i == my_k, 0, 4)
        at = first * 2 + owner % 2
        for a in range(8):

            @pl.when(array == a)
            def _():
                pltpu.make_async_copy(tgt[a].at[at], tiles.at[s], sems.at[s]).start()

        return 0

    lax.fori_loop(0, n, fetch, 0)
    for ref, places in zip(src, chunk_places(b, z)):
        for h, at in enumerate(places):
            for p in range(2):
                chunk = ref[h, p]
                raw[p, pl.ds(at, 128), :] = chunk
                unit_src[p, pl.ds(at, 128), :] = unit(chunk)
    acc[...] = jnp.zeros_like(acc)
    scale = math.log2(math.e) / (256 * TEMP)
    shift = OFFSET / TEMP * math.log2(math.e)

    def step(s, _):
        p, _ = slot_of(meta, s)
        pltpu.make_async_copy(tgt[0].at[0], tiles.at[s], sems.at[s]).wait()
        tile = unit(tiles[s])
        for c in range(4):
            cols = slice(c * 256, (c + 1) * 256)
            score = lax.dot_general(
                tile, unit_src[p, cols, :], (((1,), (1,)), ((), ())), preferred_element_type=F32
            )
            k = jnp.exp2(score * scale - shift)
            kt[s, :, cols] = k.astype(BF16)
            acc[p, :, cols] += k.reshape(16, 8, 256).sum(axis=0)
        return 0

    lax.fori_loop(0, n, step, 0)
    lane = lax.broadcasted_iota(jnp.int32, (1, 1024), 1) // 128
    for p in range(2):
        rows[p : p + 1, :] = jnp.sum(acc[p], axis=0, keepdims=True)
        own = jnp.concatenate([mass[p : p + 1, :].astype(F32)] * 8, axis=1)
        rows[2 + p : 3 + p, :] = jnp.where(lane == z, own, 0.0)


def col_kernel(first, *refs):
    meta, refs = refs[:3], refs[3:]
    if first:
        kt, r0, r1, r2, r3, tgt_mass, out, mass_out, u_rows = refs
        total = (r0[...] + r1[...]) + (r2[...] + r3[...])
        mass = total[2:4]
        mass_out[...] = mass
    else:
        kt, r0, r1, r2, r3, mass_in, out, u_out, u_rows = refs
        total = (r0[...] + r1[...]) + (r2[...] + r3[...])
        mass = mass_in[...]
    u = mass / total[0:2]
    if not first:
        u_out[...] = u
    for p in range(2):
        u_rows[p] = two_rows(u[p : p + 1])
    out[...] = jnp.zeros_like(out)

    def step(s, _):
        p, j = slot_of(meta, s)
        part = lax.dot_general(
            u_rows[p], kt[s], (((1,), (1,)), ((), ())), preferred_element_type=F32
        )
        out[pl.ds(j, 1), :] += part[0:1] + part[1:2]
        return 0

    lax.fori_loop(0, live(meta), step, 0)
    if first:
        b = place()[0]
        out[pl.ds(64 + 2 * b, 1), :] = tgt_mass[0:1, :].astype(F32)
        out[pl.ds(65 + 2 * b, 1), :] = tgt_mass[1:2, :].astype(F32)


def row_kernel(*refs):
    meta, refs = refs[:3], refs[3:]
    kt, c0, c1, c2, c3, out, mass_out, v_all, acc = refs
    total = c0[...] + c1[...].astype(F32) + c2[...].astype(F32) + c3[...].astype(F32)
    mass_out[...] = total[64:]
    v_all[...] = total[64:] / total[:64]
    acc[...] = jnp.zeros_like(acc)

    def step(s, _):
        p, j = slot_of(meta, s)
        v = two_rows(v_all[pl.ds(j, 1), :])
        acc[p] += jnp.dot(v, kt[s], preferred_element_type=F32)[:8]
        return 0

    lax.fori_loop(0, live(meta), step, 0)
    for p in range(2):
        out[p : p + 1, :] = acc[p, 0:1, :] + acc[p, 1:2, :]


def back_kernel(*refs):
    meta, refs = refs[:3], refs[3:]
    kt, u, raw, mine, other = refs
    _, _, my_y, my_x, my_k = place()
    mine[...] = jnp.zeros_like(mine)
    other[...] = jnp.zeros_like(other)

    def step(s, _):
        p, j = slot_of(meta, s)
        row = jnp.where(p == 0, u[0:1, :], u[1:2, :])
        plan = (kt[s].astype(F32) * row).astype(BF16)
        back = jnp.dot(plan, raw[p], preferred_element_type=F32)
        i, owner = j % 2, j // 2
        dy, dx = (owner // 8) ^ my_y, ((owner // 2) % 4) ^ my_x
        at = jnp.where(i == 0, dx * 8 + dy * 2, dy * 8 + dx * 2) + owner % 2

        @pl.when(i == my_k)
        def _():
            mine[at] = (mine[at].astype(F32) + back).astype(BF16)

        @pl.when(i != my_k)
        def _():
            other[at] = (other[at].astype(F32) + back).astype(BF16)

        return 0

    lax.fori_loop(0, live(meta), step, 0)


def toward_kernel(*refs):
    meta, refs = refs[:3], refs[3:]
    kt, u, tiles, c0, c1, c2, c3, mass, out1, out2, out3, out4, v_out, v_all, acc = refs
    total = c0[...] + c1[...].astype(F32) + c2[...].astype(F32) + c3[...].astype(F32)
    v_all[...] = mass[...] / total
    b, z = place()[:2]
    v_out[0:1, :] = v_all[pl.ds(2 * b, 1), :]
    v_out[1:2, :] = v_all[pl.ds(2 * b + 1, 1), :]
    acc[...] = jnp.zeros_like(acc)

    def step(s, _):
        p, j = slot_of(meta, s)
        v = jnp.broadcast_to(v_all[pl.ds(j, 1), :], (128, 128)).T
        row = jnp.where(p == 0, u[0:1, :], u[1:2, :])
        plan = []
        for c in range(8):
            cols = slice(c * 128, (c + 1) * 128)
            plan.append((kt[s, :, cols].astype(F32) * row[:, cols] * v).astype(BF16))
        plan = jnp.concatenate(plan, axis=1)
        acc[p] += lax.dot_general(
            plan, tiles[s], (((0,), (0,)), ((), ())), preferred_element_type=F32
        )
        return 0

    lax.fori_loop(0, live(meta), step, 0)
    for ref, places in zip((out1, out2, out3, out4), chunk_places(b, z)):
        for h, at in enumerate(places):
            for p in range(2):
                ref[h, p] = acc[p, pl.ds(at, 128), :].astype(BF16)


def call(kernel, out_shape, in_specs, scratch, args, flops, nbytes):
    return pl.pallas_call(
        kernel,
        out_shape=out_shape,
        in_specs=in_specs,
        out_specs=[VMEM] * len(out_shape),
        scratch_shapes=scratch,
        compiler_params=pltpu.CompilerParams(vmem_limit_bytes=LIMIT),
        cost_estimate=pl.CostEstimate(flops=flops, bytes_accessed=nbytes, transcendentals=0),
    )(*args)


def program(src_feat, tgt_feat, src_mass, tgt_mass, candidates, counts, tgt_home):
    core = lax.axis_index("blk") % 2
    meta = (counts, candidates, tgt_home)
    even = (lax.axis_index("col") + core) % 2 == 0
    sources = gather_sources(src_feat, even)
    targets = gather_targets(tgt_feat, core)
    S = jax.ShapeDtypeStruct
    kt, tiles, raw, rows = call(
        build_kernel,
        [
            S((PAIRS, 128, 1024), BF16),
            S((PAIRS, 128, 256), BF16),
            S((2, 1024, 256), BF16),
            S((4, 1024), F32),
        ],
        [SMEM] * 3 + [VMEM] * 4 + [ANY] * 8 + [VMEM],
        [
            pltpu.VMEM((2, 1024, 256), BF16),
            pltpu.VMEM((2, 8, 1024), F32),
            pltpu.SemaphoreType.DMA((PAIRS,)),
        ],
        (*meta, *sources, *targets, src_mass),
        800_000_000,
        7_000_000,
    )
    sums, mass_src = call(
        functools.partial(col_kernel, True),
        [S((128, 128), F32), S((2, 1024), F32)],
        [SMEM] * 3 + [VMEM] * 6,
        [pltpu.VMEM((2, 16, 1024), BF16)],
        (*meta, kt, *col_sum_parts(rows), tgt_mass),
        100_000_000,
        3_000_000,
    )
    rows, mass_tgt = call(
        row_kernel,
        [S((2, 1024), F32), S((64, 128), F32)],
        [SMEM] * 3 + [VMEM] * 5,
        [pltpu.VMEM((64, 128), F32), pltpu.VMEM((2, 8, 1024), F32)],
        (*meta, kt, *blk_sum_parts(sums)),
        100_000_000,
        3_000_000,
    )
    sums, u = call(
        functools.partial(col_kernel, False),
        [S((64, 128), F32), S((2, 1024), F32)],
        [SMEM] * 3 + [VMEM] * 6,
        [pltpu.VMEM((2, 16, 1024), BF16)],
        (*meta, kt, *col_sum_parts(rows), mass_src),
        100_000_000,
        3_000_000,
    )
    mine, other = call(
        back_kernel,
        [S((32, 128, 256), BF16)] * 2,
        [SMEM] * 3 + [VMEM] * 3,
        [],
        (*meta, kt, u, raw),
        800_000_000,
        8_000_000,
    )
    came = swap(other)
    parts = blk_sum_parts(sums)
    tgt_own = reduce_targets(mine, came, core)
    *parts, v = call(
        toward_kernel,
        [S((2, 2, 128, 256), BF16)] * 4 + [S((2, 128), F32)],
        [SMEM] * 3 + [VMEM] * 8,
        [pltpu.VMEM((64, 128), F32), pltpu.VMEM((2, 1024, 256), F32)],
        (*meta, kt, u, tiles, *parts, mass_tgt),
        800_000_000,
        6_000_000,
    )
    src_own = reduce_sources(parts, even)
    src_aligned = (src_own / src_mass.astype(F32)[:, :, None]).astype(BF16)
    tgt_aligned = (tgt_own * v[:, :, None] / tgt_mass.astype(F32)[:, :, None]).astype(BF16)
    return (src_aligned, tgt_aligned)


def solution(mesh):
    in_specs = (
        P("blk", "col", None),
        P("blk", "col", None),
        P("blk", "col"),
        P("blk", "col"),
        P("blk", None),
        P("blk"),
        P(),
    )
    out_specs = (P("blk", "col", None), P("blk", "col", None))
    return jax.shard_map(program, mesh=mesh, in_specs=in_specs, out_specs=out_specs, check_vma=False)
```

```python
import functools
import math

import jax
import jax.numpy as jnp
from jax import lax
from jax.experimental import pallas as pl
from jax.experimental.pallas import tpu as pltpu
from jax.sharding import PartitionSpec as P


GROUPS = 7
TEMP = 0.02
OFFSET = 0.3
EPS = 1e-06
F32 = jnp.float32
BF16 = jnp.bfloat16
SMEM = pl.BlockSpec(memory_space=pltpu.SMEM)
VMEM = pl.BlockSpec(memory_space=pltpu.VMEM)
ANY = pl.BlockSpec(memory_space=pl.ANY)
LIMIT = 16 * 1024 * 1024


def blk_perm(fn):
    pairs = []
    for i in range(32):
        y, x, k = fn(i // 8, (i // 2) % 4, i % 2)
        pairs.append((i, (y * 4 + x) * 2 + k))
    return pairs


def swap(v):
    return lax.ppermute(v, "blk", blk_perm(lambda y, x, k: (y, x, 1 - k)))


def over_x(v, d):
    return lax.ppermute(v, "blk", blk_perm(lambda y, x, k: (y, x ^ d, k)))


def over_y(v, d):
    return lax.ppermute(v, "blk", blk_perm(lambda y, x, k: (y ^ d, x, k)))


def over_first(v, d):
    return lax.ppermute(
        v, "blk", blk_perm(lambda y, x, k: (y, x ^ d, k) if k == 0 else (y ^ d, x, k))
    )


def over_second(v, d):
    return lax.ppermute(
        v, "blk", blk_perm(lambda y, x, k: (y ^ d, x, k) if k == 0 else (y, x ^ d, k))
    )


def over_z(v, d):
    return lax.ppermute(v, "col", [(i, i ^ d) for i in range(8)])


def along_z(v, odd):
    pairs = []
    for i in range(256):
        z, core = i % 8, (i // 8) % 2
        pairs.append((i, i - z + (((z + core + odd) ^ 1) - core - odd) % 8))
    return lax.ppermute(v, ("blk", "col"), pairs)


def pick(core, zero, one):
    return jnp.where(core == 0, zero, one)


def gather_targets(tgt_feat, core):
    came = swap(tgt_feat)
    pair = pick(core, jnp.stack([tgt_feat[0], came[0]]), jnp.stack([came[1], tgt_feat[1]]))
    near = [pair]
    for d in (1, 2, 3):
        near.append(over_first(pair, d))
    near = jnp.concatenate(near)
    parts = [near]
    for d in (1, 2, 3):
        parts.append(over_second(near, d))
    for n in range(4):
        parts.append(swap(parts[n]))
    return parts


def gather_sources(src_feat, even):
    came = along_z(src_feat, 0)
    pairs = [jnp.where(even, jnp.stack([src_feat, came]), jnp.stack([came, src_feat]))]
    for step in (2, 3, 4):
        pairs.append(along_z(pairs[-1], (step + 1) % 2))
    return pairs


def col_sum_parts(v):
    v = v + over_z(v.astype(BF16), 1).astype(F32)
    low = v.astype(BF16)
    return (v,) + tuple(over_z(low, d) for d in (5, 2, 6))


def blk_sum_parts(v):
    v = v + swap(v.astype(BF16)).astype(F32)
    low = v.astype(BF16)
    for d in (1, 3, 2):
        v = v + over_x(low, d).astype(F32)
    low = v.astype(BF16)
    parts = [v]
    for d in (1, 3, 2):
        parts.append(over_y(low, d))
    return parts


def reduce_targets(mine, came, core):
    q = (mine.astype(F32) + came.astype(F32)).astype(BF16).reshape(4, 8, 128, 256)
    s = q[0].astype(F32)
    for d in (1, 3, 2):
        s = s + over_first(q[d], d).astype(F32)
    s = s.astype(BF16).reshape(4, 2, 128, 256)
    t = s[0].astype(F32)
    for d in (1, 3, 2):
        came = over_second(s[d], d)
        t = t + came.astype(F32)
    keep = pick(core, t[0], t[1])
    came = swap(pick(core, t[1], t[0]).astype(BF16)).astype(F32)
    return pick(core, jnp.stack([keep, came]), jnp.stack([came, keep]))


def reduce_sources(parts, even):
    moving = along_z(parts[3], 1)
    for step in (2, 1):
        moving = along_z((parts[step].astype(F32) + moving.astype(F32)).astype(BF16), step % 2)
    pair = parts[0].astype(F32) + moving.astype(F32)
    came = along_z(jnp.where(even, pair[1], pair[0]).astype(BF16), 0)
    return jnp.where(even, pair[0], pair[1]) + came.astype(F32)


def group_of(meta, g):
    counts, candidates, home = meta
    first = lax.shift_right_logical(counts[0] + 1, 1)
    p = jnp.where(g >= first, 1, 0)
    k = jnp.minimum(2 * (g - first * p), 6)
    both = k + 1 < counts[p]
    return p, (home[candidates[p, k]], home[candidates[p, jnp.where(both, k + 1, k)]]), both


def live(meta):
    counts = meta[0]
    return lax.shift_right_logical(counts[0] + 1, 1) + lax.shift_right_logical(counts[1] + 1, 1)


def place():
    b = lax.axis_index("blk")
    return b, lax.axis_index("col"), b // 8, (b // 2) % 4, b % 2


def chunk_places(b, z):
    core = b % 2
    half = (z + core) & 7
    way = 1 - 2 * (half % 2)
    places = []
    for off in (0, -way, way, 2):
        first = 2 * (half // 2 + off)
        places.append([pl.multiple_of(((first + h - core) & 7) * 128, 128) for h in range(2)])
    return places


def unit(rows):
    x = rows.astype(F32)
    return (x * lax.rsqrt(jnp.mean(x * x, axis=-1, keepdims=True) + EPS)).astype(BF16)


def two_rows(v):
    high = v.astype(BF16).astype(F32)
    row = lax.broadcasted_iota(jnp.int32, (16, v.shape[1]), 0)
    return jnp.where(row == 0, high, jnp.where(row == 1, v - high, 0.0)).astype(BF16)


def unit_kernel(s0, s1, s2, s3, raw, unit_src):
    b, z = place()[:2]
    for ref, places in zip((s0, s1, s2, s3), chunk_places(b, z)):
        for h, at in enumerate(places):
            for p in range(2):
                chunk = ref[h, p]
                raw[p, pl.ds(at, 128), :] = chunk
                unit_src[p, pl.ds(at, 128), :] = unit(chunk)


def build_kernel(*refs):
    meta, refs = refs[:3], refs[3:]
    tgt = refs[:8]
    unit_src, mass, kt, tiles, rows, acc, sems = refs[8:]
    n = live(meta)
    _, z, my_y, my_x, my_k = place()

    def fetch(g, _):
        _, targets, _ = group_of(meta, g)
        for h, j in enumerate(targets):
            i, owner = j % 2, j // 2
            dy, dx = (owner // 8) ^ my_y, ((owner // 2) % 4) ^ my_x
            first, second = jnp.where(i == 0, dx, dy), jnp.where(i == 0, dy, dx)
            array = second + jnp.where(i == my_k, 0, 4)
            at = first * 2 + owner % 2
            for a in range(8):

                @pl.when(array == a)
                def _():
                    pltpu.make_async_copy(
                        tgt[a].at[at], tiles.at[g, pl.ds(h * 128, 128), :], sems.at[g, h]
                    ).start()

        return 0

    lax.fori_loop(0, n, fetch, 0)
    acc[...] = jnp.zeros_like(acc)
    scale = math.log2(math.e) / (256 * TEMP)
    shift = OFFSET / TEMP * math.log2(math.e)

    def step(g, _):
        p, _, both = group_of(meta, g)
        for h in range(2):
            pltpu.make_async_copy(
                tgt[0].at[0], tiles.at[g, pl.ds(h * 128, 128), :], sems.at[g, h]
            ).wait()
        tile = unit(tiles[g])
        keep = jnp.where(both, 1.0, 0.0)
        for c in range(4):
            cols = slice(c * 256, (c + 1) * 256)
            score = lax.dot_general(
                tile, unit_src[p, cols, :], (((1,), (1,)), ((), ())), preferred_element_type=F32
            )
            k = jnp.exp2(score * scale - shift)
            upper, lower = k[:128], k[128:] * keep
            kt[g, :128, cols] = upper.astype(BF16)
            kt[g, 128:, cols] = lower.astype(BF16)
            acc[p, :, cols] += (upper + lower).reshape(16, 8, 256).sum(axis=0)
        return 0

    lax.fori_loop(0, n, step, 0)

    def clear(g, _):
        kt[g] = jnp.zeros_like(kt[g])
        return 0

    lax.fori_loop(n, GROUPS, clear, 0)
    lane = lax.broadcasted_iota(jnp.int32, (1, 1024), 1) // 128
    for p in range(2):
        rows[p : p + 1, :] = jnp.sum(acc[p], axis=0, keepdims=True)
        own = jnp.concatenate([mass[p : p + 1, :].astype(F32)] * 8, axis=1)
        rows[2 + p : 3 + p, :] = jnp.where(lane == z, own, 0.0)


def col_kernel(first, *refs):
    meta, refs = refs[:3], refs[3:]
    if first:
        kt, r0, r1, r2, r3, tgt_mass, out, mass_out, u_rows = refs
        total = r0[...] + r1[...].astype(F32) + r2[...].astype(F32) + r3[...].astype(F32)
        mass = total[2:4]
        mass_out[...] = mass
    else:
        kt, r0, r1, r2, r3, mass_in, out, u_out, u_rows = refs
        total = r0[...] + r1[...].astype(F32) + r2[...].astype(F32) + r3[...].astype(F32)
        mass = mass_in[...]
    u = mass / total[0:2]
    if not first:
        u_out[...] = u
    for p in range(2):
        u_rows[p] = two_rows(u[p : p + 1])
    out[...] = jnp.zeros_like(out)

    found = []
    for g in range(GROUPS):
        p, targets, _ = group_of(meta, g)
        part = lax.dot_general(
            u_rows[p], kt[g], (((1,), (1,)), ((), ())), preferred_element_type=F32
        )
        found.append((targets, part[0:1] + part[1:2]))
    for targets, part in found:
        for h, j in enumerate(targets):
            out[pl.ds(j, 1), :] += part[:, h * 128 : (h + 1) * 128]
    if first:
        b = place()[0]
        out[pl.ds(64 + 2 * b, 1), :] = tgt_mass[0:1, :].astype(F32)
        out[pl.ds(65 + 2 * b, 1), :] = tgt_mass[1:2, :].astype(F32)


def row_kernel(*refs):
    meta, refs = refs[:3], refs[3:]
    kt, c0, c1, c2, c3, out, mass_out, v_all, acc = refs
    total = c0[...] + c1[...].astype(F32) + c2[...].astype(F32) + c3[...].astype(F32)
    mass_out[...] = total[64:]
    v_all[...] = total[64:] / total[:64]
    acc[...] = jnp.zeros_like(acc)

    found = []
    for g in range(GROUPS):
        p, targets, _ = group_of(meta, g)
        v = two_rows(jnp.concatenate([v_all[pl.ds(j, 1), :] for j in targets], axis=1))
        found.append((p, jnp.dot(v, kt[g], preferred_element_type=F32)[:8]))
    for p, part in found:
        acc[p] += part
    for p in range(2):
        out[p : p + 1, :] = acc[p, 0:1, :] + acc[p, 1:2, :]


def back_kernel(*refs):
    meta, refs = refs[:3], refs[3:]
    kt, u, raw, mine, other = refs
    _, _, my_y, my_x, my_k = place()
    mine[...] = jnp.zeros_like(mine)
    other[...] = jnp.zeros_like(other)

    def step(g, _):
        p, targets, _ = group_of(meta, g)
        row = jnp.where(p == 0, u[0:1, :], u[1:2, :])
        plan = (kt[g].astype(F32) * row).astype(BF16)
        both = jnp.dot(plan, raw[p], preferred_element_type=F32)
        for h, j in enumerate(targets):
            back = both[h * 128 : (h + 1) * 128]
            i, owner = j % 2, j // 2
            dy, dx = (owner // 8) ^ my_y, ((owner // 2) % 4) ^ my_x
            at = jnp.where(i == 0, dx * 8 + dy * 2, dy * 8 + dx * 2) + owner % 2

            @pl.when(i == my_k)
            def _():
                mine[at] = (mine[at].astype(F32) + back).astype(BF16)

            @pl.when(i != my_k)
            def _():
                other[at] = (other[at].astype(F32) + back).astype(BF16)

        return 0

    lax.fori_loop(0, live(meta), step, 0)


def toward_kernel(*refs):
    meta, refs = refs[:3], refs[3:]
    kt, u, tiles, c0, c1, c2, c3, mass, out1, out2, out3, out4, v_out, v_all, acc = refs
    total = c0[...] + c1[...].astype(F32) + c2[...].astype(F32) + c3[...].astype(F32)
    v_all[...] = mass[...] / total
    b, z = place()[:2]
    v_out[0:1, :] = v_all[pl.ds(2 * b, 1), :]
    v_out[1:2, :] = v_all[pl.ds(2 * b + 1, 1), :]
    acc[...] = jnp.zeros_like(acc)

    def step(g, _):
        p, targets, _ = group_of(meta, g)
        v = [jnp.broadcast_to(v_all[pl.ds(j, 1), :], (128, 128)).T for j in targets]
        v = jnp.concatenate(v, axis=0)
        row = jnp.where(p == 0, u[0:1, :], u[1:2, :])
        tile = tiles[g].T
        for c in range(4):
            plan = []
            for d in range(2):
                cols = slice(c * 256 + d * 128, c * 256 + (d + 1) * 128)
                plan.append((kt[g, :, cols].astype(F32) * row[:, cols] * v).astype(BF16))
            cols = slice(c * 256, (c + 1) * 256)
            acc[p, :, cols] += jnp.dot(
                tile, jnp.concatenate(plan, axis=1), preferred_element_type=F32
            )
        return 0

    lax.fori_loop(0, live(meta), step, 0)
    for ref, places in zip((out1, out2, out3, out4), chunk_places(b, z)):
        for h, at in enumerate(places):
            for p in range(2):
                ref[h, p] = acc[p, :, pl.ds(at, 128)].astype(BF16).T


def call(kernel, out_shape, in_specs, scratch, args, flops, nbytes):
    return pl.pallas_call(
        kernel,
        out_shape=out_shape,
        in_specs=in_specs,
        out_specs=[VMEM] * len(out_shape),
        scratch_shapes=scratch,
        compiler_params=pltpu.CompilerParams(vmem_limit_bytes=LIMIT),
        cost_estimate=pl.CostEstimate(flops=flops, bytes_accessed=nbytes, transcendentals=0),
    )(*args)


def program(src_feat, tgt_feat, src_mass, tgt_mass, candidates, counts, tgt_home):
    core = lax.axis_index("blk") % 2
    meta = (counts, candidates, tgt_home)
    even = (lax.axis_index("col") + core) % 2 == 0
    sources = gather_sources(src_feat, even)
    targets = gather_targets(tgt_feat, core)
    S = jax.ShapeDtypeStruct
    raw, unit_src = call(
        unit_kernel, [S((2, 1024, 256), BF16)] * 2, [VMEM] * 4, [], sources, 2_000_000, 3_000_000
    )
    kt, tiles, rows = call(
        build_kernel,
        [S((GROUPS, 256, 1024), BF16), S((GROUPS, 256, 256), BF16), S((4, 1024), F32)],
        [SMEM] * 3 + [ANY] * 8 + [VMEM] * 2,
        [pltpu.VMEM((2, 8, 1024), F32), pltpu.SemaphoreType.DMA((GROUPS, 2))],
        (*meta, *targets, unit_src, src_mass),
        800_000_000,
        7_000_000,
    )
    sums, mass_src = call(
        functools.partial(col_kernel, True),
        [S((128, 128), F32), S((2, 1024), F32)],
        [SMEM] * 3 + [VMEM] * 6,
        [pltpu.VMEM((2, 16, 1024), BF16)],
        (*meta, kt, *col_sum_parts(rows), tgt_mass),
        100_000_000,
        3_000_000,
    )
    rows, mass_tgt = call(
        row_kernel,
        [S((2, 1024), F32), S((64, 128), F32)],
        [SMEM] * 3 + [VMEM] * 5,
        [pltpu.VMEM((64, 128), F32), pltpu.VMEM((2, 8, 1024), F32)],
        (*meta, kt, *blk_sum_parts(sums)),
        100_000_000,
        3_000_000,
    )
    sums, u = call(
        functools.partial(col_kernel, False),
        [S((64, 128), F32), S((2, 1024), F32)],
        [SMEM] * 3 + [VMEM] * 6,
        [pltpu.VMEM((2, 16, 1024), BF16)],
        (*meta, kt, *col_sum_parts(rows), mass_src),
        100_000_000,
        3_000_000,
    )
    mine, other = call(
        back_kernel,
        [S((32, 128, 256), BF16)] * 2,
        [SMEM] * 3 + [VMEM] * 3,
        [],
        (*meta, kt, u, raw),
        800_000_000,
        8_000_000,
    )
    came = swap(other)
    parts = blk_sum_parts(sums)
    tgt_own = reduce_targets(mine, came, core)
    *parts, v = call(
        toward_kernel,
        [S((2, 2, 128, 256), BF16)] * 4 + [S((2, 128), F32)],
        [SMEM] * 3 + [VMEM] * 8,
        [pltpu.VMEM((64, 128), F32), pltpu.VMEM((2, 256, 1024), F32)],
        (*meta, kt, u, tiles, *parts, mass_tgt),
        800_000_000,
        6_000_000,
    )
    src_own = reduce_sources(parts, even)
    src_aligned = (src_own / src_mass.astype(F32)[:, :, None]).astype(BF16)
    tgt_aligned = (tgt_own * v[:, :, None] / tgt_mass.astype(F32)[:, :, None]).astype(BF16)
    return (src_aligned, tgt_aligned)


def solution(mesh):
    in_specs = (
        P("blk", "col", None),
        P("blk", "col", None),
        P("blk", "col"),
        P("blk", "col"),
        P("blk", None),
        P("blk"),
        P(),
    )
    out_specs = (P("blk", "col", None), P("blk", "col", None))
    return jax.shard_map(program, mesh=mesh, in_specs=in_specs, out_specs=out_specs, check_vma=False)
```

```python
import functools
import math

import jax
import jax.numpy as jnp
from jax import lax
from jax.experimental import pallas as pl
from jax.experimental.pallas import tpu as pltpu
from jax.sharding import PartitionSpec as P


GROUPS = 7
TEMP = 0.02
OFFSET = 0.3
EPS = 1e-06
F32 = jnp.float32
BF16 = jnp.bfloat16
SMEM = pl.BlockSpec(memory_space=pltpu.SMEM)
VMEM = pl.BlockSpec(memory_space=pltpu.VMEM)
LIMIT = 16 * 1024 * 1024


def blk_perm(fn):
    pairs = []
    for i in range(32):
        y, x, k = fn(i // 8, (i // 2) % 4, i % 2)
        pairs.append((i, (y * 4 + x) * 2 + k))
    return pairs


def swap(v):
    return lax.ppermute(v, "blk", blk_perm(lambda y, x, k: (y, x, 1 - k)))


def over_x(v, d):
    return lax.ppermute(v, "blk", blk_perm(lambda y, x, k: (y, x ^ d, k)))


def over_y(v, d):
    return lax.ppermute(v, "blk", blk_perm(lambda y, x, k: (y ^ d, x, k)))


def over_first(v, d):
    return lax.ppermute(
        v, "blk", blk_perm(lambda y, x, k: (y, x ^ d, k) if k == 0 else (y ^ d, x, k))
    )


def over_second(v, d):
    return lax.ppermute(
        v, "blk", blk_perm(lambda y, x, k: (y ^ d, x, k) if k == 0 else (y, x ^ d, k))
    )


def over_z(v, d):
    return lax.ppermute(v, "col", [(i, i ^ d) for i in range(8)])


def along_z(v, odd):
    pairs = []
    for i in range(256):
        z, core = i % 8, (i // 8) % 2
        pairs.append((i, i - z + (((z + core + odd) ^ 1) - core - odd) % 8))
    return lax.ppermute(v, ("blk", "col"), pairs)


def pick(core, zero, one):
    return jnp.where(core == 0, zero, one)


def gather_targets(tgt_feat, core):
    came = swap(tgt_feat)
    pair = pick(core, jnp.stack([tgt_feat[0], came[0]]), jnp.stack([came[1], tgt_feat[1]]))
    near = [pair]
    for d in (1, 2, 3):
        near.append(over_first(pair, d))
    near = jnp.concatenate(near)
    parts = [near]
    for d in (1, 2, 3):
        parts.append(over_second(near, d))
    for n in range(4):
        parts.append(swap(parts[n]))
    return parts


def gather_sources(src_feat, even):
    came = along_z(src_feat, 0)
    pairs = [jnp.where(even, jnp.stack([src_feat, came]), jnp.stack([came, src_feat]))]
    for step in (2, 3, 4):
        pairs.append(along_z(pairs[-1], (step + 1) % 2))
    return pairs


def col_sum_parts(v):
    v = v + over_z(v.astype(BF16), 1).astype(F32)
    low = v.astype(BF16)
    return (v,) + tuple(over_z(low, d) for d in (5, 2, 6))


def blk_sum_parts(v):
    v = v + swap(v.astype(BF16)).astype(F32)
    low = v.astype(BF16)
    for d in (1, 3, 2):
        v = v + over_x(low, d).astype(F32)
    low = v.astype(BF16)
    parts = [v]
    for d in (1, 3, 2):
        parts.append(over_y(low, d))
    return parts


def reduce_targets(mine, came, core):
    q = (mine.astype(F32) + came.astype(F32)).astype(BF16).reshape(4, 8, 128, 256)
    s = q[0].astype(F32)
    for d in (1, 3, 2):
        s = s + over_first(q[d], d).astype(F32)
    s = s.astype(BF16).reshape(4, 2, 128, 256)
    t = s[0].astype(F32)
    for d in (1, 3, 2):
        came = over_second(s[d], d)
        t = t + came.astype(F32)
    keep = pick(core, t[0], t[1])
    came = swap(pick(core, t[1], t[0]).astype(BF16)).astype(F32)
    return pick(core, jnp.stack([keep, came]), jnp.stack([came, keep]))


def reduce_sources(parts, even):
    moving = along_z(parts[3], 1)
    for step in (2, 1):
        moving = along_z((parts[step].astype(F32) + moving.astype(F32)).astype(BF16), step % 2)
    pair = parts[0].astype(F32) + moving.astype(F32)
    came = along_z(jnp.where(even, pair[1], pair[0]).astype(BF16), 0)
    return jnp.where(even, pair[0], pair[1]) + came.astype(F32)


def group_of(meta, g):
    counts, candidates, home = meta
    first = lax.shift_right_logical(counts[0] + 1, 1)
    p = jnp.where(g >= first, 1, 0)
    k = jnp.minimum(2 * (g - first * p), 6)
    both = k + 1 < counts[p]
    return p, (home[candidates[p, k]], home[candidates[p, jnp.where(both, k + 1, k)]]), both


def live(meta):
    counts = meta[0]
    return lax.shift_right_logical(counts[0] + 1, 1) + lax.shift_right_logical(counts[1] + 1, 1)


def place():
    b = lax.axis_index("blk")
    return b, lax.axis_index("col"), b // 8, (b // 2) % 4, b % 2


def chunk_places(b, z):
    core = b % 2
    half = (z + core) & 7
    way = 1 - 2 * (half % 2)
    places = []
    for off in (0, -way, way, 2):
        first = 2 * (half // 2 + off)
        places.append([pl.multiple_of(((first + h - core) & 7) * 128, 128) for h in range(2)])
    return places


def unit(rows):
    x = rows.astype(F32)
    return (x * lax.rsqrt(jnp.mean(x * x, axis=-1, keepdims=True) + EPS)).astype(BF16)


def two_rows(v):
    high = v.astype(BF16).astype(F32)
    row = lax.broadcasted_iota(jnp.int32, (16, v.shape[1]), 0)
    return jnp.where(row == 0, high, jnp.where(row == 1, v - high, 0.0)).astype(BF16)


def unit_kernel(s0, s1, s2, s3, raw, unit_src):
    b, z = place()[:2]
    for ref, places in zip((s0, s1, s2, s3), chunk_places(b, z)):
        for h, at in enumerate(places):
            for p in range(2):
                chunk = ref[h, p]
                raw[p, pl.ds(at, 128), :] = chunk
                unit_src[p, pl.ds(at, 128), :] = unit(chunk)


def build_kernel(*refs):
    meta, refs = refs[:3], refs[3:]
    tgt = refs[:8]
    unit_src, mass, kt, tiles, rows, acc = refs[8:]
    n = live(meta)
    _, z, my_y, my_x, my_k = place()

    def fetch(g, targets):
        for h, j in enumerate(targets):
            i, owner = j % 2, j // 2
            dy, dx = (owner // 8) ^ my_y, ((owner // 2) % 4) ^ my_x
            first, second = jnp.where(i == 0, dx, dy), jnp.where(i == 0, dy, dx)
            at = first * 2 + owner % 2
            for near in (0, 1):

                @pl.when((i == my_k) == (near == 0))
                def _():
                    for a in range(4):

                        @pl.when(second == a)
                        def _():
                            tiles[g, h * 128 : (h + 1) * 128, :] = tgt[4 * near + a][at]

    acc[...] = jnp.zeros_like(acc)
    scale = math.log2(math.e) / (256 * TEMP)
    shift = OFFSET / TEMP * math.log2(math.e)

    def step(g, _):
        p, targets, both = group_of(meta, g)
        fetch(g, targets)
        tile = unit(tiles[g])
        keep = jnp.where(both, 1.0, 0.0)
        for c in range(4):
            cols = slice(c * 256, (c + 1) * 256)
            score = lax.dot_general(
                tile, unit_src[p, cols, :], (((1,), (1,)), ((), ())), preferred_element_type=F32
            )
            k = jnp.exp2(score * scale - shift)
            upper, lower = k[:128], k[128:] * keep
            kt[g, :128, cols] = upper.astype(BF16)
            kt[g, 128:, cols] = lower.astype(BF16)
            acc[p, :, cols] += (upper + lower).reshape(16, 8, 256).sum(axis=0)
        return 0

    lax.fori_loop(0, n, step, 0)

    def clear(g, _):
        kt[g] = jnp.zeros_like(kt[g])
        return 0

    lax.fori_loop(n, GROUPS, clear, 0)
    lane = lax.broadcasted_iota(jnp.int32, (1, 1024), 1) // 128
    for p in range(2):
        rows[p : p + 1, :] = jnp.sum(acc[p], axis=0, keepdims=True)
        own = jnp.concatenate([mass[p : p + 1, :].astype(F32)] * 8, axis=1)
        rows[2 + p : 3 + p, :] = jnp.where(lane == z, own, 0.0)


def col_kernel(first, *refs):
    meta, refs = refs[:3], refs[3:]
    if first:
        kt, r0, r1, r2, r3, tgt_mass, out, mass_out, u_rows = refs
        total = r0[...] + r1[...].astype(F32) + r2[...].astype(F32) + r3[...].astype(F32)
        mass = total[2:4]
        mass_out[...] = mass
    else:
        kt, r0, r1, r2, r3, mass_in, out, u_out, u_rows = refs
        total = r0[...] + r1[...].astype(F32) + r2[...].astype(F32) + r3[...].astype(F32)
        mass = mass_in[...]
    u = mass / total[0:2]
    if not first:
        u_out[...] = u
    for p in range(2):
        u_rows[p] = two_rows(u[p : p + 1])
    out[...] = jnp.zeros_like(out)

    found = []
    for g in range(GROUPS):
        p, targets, _ = group_of(meta, g)
        part = lax.dot_general(
            u_rows[p], kt[g], (((1,), (1,)), ((), ())), preferred_element_type=F32
        )
        found.append((targets, part[0:1] + part[1:2]))
    for targets, part in found:
        for h, j in enumerate(targets):
            out[pl.ds(j, 1), :] += part[:, h * 128 : (h + 1) * 128]
    if first:
        b = place()[0]
        out[pl.ds(64 + 2 * b, 1), :] = tgt_mass[0:1, :].astype(F32)
        out[pl.ds(65 + 2 * b, 1), :] = tgt_mass[1:2, :].astype(F32)


def row_kernel(*refs):
    meta, refs = refs[:3], refs[3:]
    kt, c0, c1, c2, c3, out, mass_out, v_all, acc = refs
    total = c0[...] + c1[...].astype(F32) + c2[...].astype(F32) + c3[...].astype(F32)
    mass_out[...] = total[64:]
    v_all[...] = total[64:] / total[:64]
    acc[...] = jnp.zeros_like(acc)

    found = []
    for g in range(GROUPS):
        p, targets, _ = group_of(meta, g)
        v = two_rows(jnp.concatenate([v_all[pl.ds(j, 1), :] for j in targets], axis=1))
        found.append((p, jnp.dot(v, kt[g], preferred_element_type=F32)[:8]))
    for p, part in found:
        acc[p] += part
    for p in range(2):
        out[p : p + 1, :] = acc[p, 0:1, :] + acc[p, 1:2, :]


def back_kernel(*refs):
    meta, refs = refs[:3], refs[3:]
    kt, u, raw, mine, other = refs
    _, _, my_y, my_x, my_k = place()
    mine[...] = jnp.zeros_like(mine)
    other[...] = jnp.zeros_like(other)

    def step(g, _):
        p, targets, _ = group_of(meta, g)
        row = jnp.where(p == 0, u[0:1, :], u[1:2, :])
        plan = (kt[g].astype(F32) * row).astype(BF16)
        both = jnp.dot(plan, raw[p], preferred_element_type=F32)
        for h, j in enumerate(targets):
            back = both[h * 128 : (h + 1) * 128]
            i, owner = j % 2, j // 2
            dy, dx = (owner // 8) ^ my_y, ((owner // 2) % 4) ^ my_x
            at = jnp.where(i == 0, dx * 8 + dy * 2, dy * 8 + dx * 2) + owner % 2

            @pl.when(i == my_k)
            def _():
                mine[at] = (mine[at].astype(F32) + back).astype(BF16)

            @pl.when(i != my_k)
            def _():
                other[at] = (other[at].astype(F32) + back).astype(BF16)

        return 0

    lax.fori_loop(0, live(meta), step, 0)


def toward_kernel(*refs):
    meta, refs = refs[:3], refs[3:]
    kt, u, tiles, c0, c1, c2, c3, mass, out1, out2, out3, out4, v_out, v_all, acc = refs
    total = c0[...] + c1[...].astype(F32) + c2[...].astype(F32) + c3[...].astype(F32)
    v_all[...] = mass[...] / total
    b, z = place()[:2]
    v_out[0:1, :] = v_all[pl.ds(2 * b, 1), :]
    v_out[1:2, :] = v_all[pl.ds(2 * b + 1, 1), :]
    acc[...] = jnp.zeros_like(acc)

    def step(g, _):
        p, targets, _ = group_of(meta, g)
        v = [jnp.broadcast_to(v_all[pl.ds(j, 1), :], (128, 128)).T for j in targets]
        v = jnp.concatenate(v, axis=0)
        row = jnp.where(p == 0, u[0:1, :], u[1:2, :])
        tile = tiles[g].T
        for c in range(4):
            plan = []
            for d in range(2):
                cols = slice(c * 256 + d * 128, c * 256 + (d + 1) * 128)
                plan.append((kt[g, :, cols].astype(F32) * row[:, cols] * v).astype(BF16))
            cols = slice(c * 256, (c + 1) * 256)
            acc[p, :, cols] += jnp.dot(
                tile, jnp.concatenate(plan, axis=1), preferred_element_type=F32
            )
        return 0

    lax.fori_loop(0, live(meta), step, 0)
    for ref, places in zip((out1, out2, out3, out4), chunk_places(b, z)):
        for h, at in enumerate(places):
            for p in range(2):
                ref[h, p] = acc[p, :, pl.ds(at, 128)].astype(BF16).T


def call(kernel, out_shape, in_specs, scratch, args, flops, nbytes):
    return pl.pallas_call(
        kernel,
        out_shape=out_shape,
        in_specs=in_specs,
        out_specs=[VMEM] * len(out_shape),
        scratch_shapes=scratch,
        compiler_params=pltpu.CompilerParams(vmem_limit_bytes=LIMIT),
        cost_estimate=pl.CostEstimate(flops=flops, bytes_accessed=nbytes, transcendentals=0),
    )(*args)


def program(src_feat, tgt_feat, src_mass, tgt_mass, candidates, counts, tgt_home):
    core = lax.axis_index("blk") % 2
    meta = (counts, candidates, tgt_home)
    even = (lax.axis_index("col") + core) % 2 == 0
    sources = gather_sources(src_feat, even)
    targets = gather_targets(tgt_feat, core)
    S = jax.ShapeDtypeStruct
    raw, unit_src = call(
        unit_kernel, [S((2, 1024, 256), BF16)] * 2, [VMEM] * 4, [], sources, 2_000_000, 3_000_000
    )
    kt, tiles, rows = call(
        build_kernel,
        [S((GROUPS, 256, 1024), BF16), S((GROUPS, 256, 256), BF16), S((4, 1024), F32)],
        [SMEM] * 3 + [VMEM] * 10,
        [pltpu.VMEM((2, 8, 1024), F32)],
        (*meta, *targets, unit_src, src_mass),
        800_000_000,
        7_000_000,
    )
    sums, mass_src = call(
        functools.partial(col_kernel, True),
        [S((128, 128), F32), S((2, 1024), F32)],
        [SMEM] * 3 + [VMEM] * 6,
        [pltpu.VMEM((2, 16, 1024), BF16)],
        (*meta, kt, *col_sum_parts(rows), tgt_mass),
        100_000_000,
        3_000_000,
    )
    rows, mass_tgt = call(
        row_kernel,
        [S((2, 1024), F32), S((64, 128), F32)],
        [SMEM] * 3 + [VMEM] * 5,
        [pltpu.VMEM((64, 128), F32), pltpu.VMEM((2, 8, 1024), F32)],
        (*meta, kt, *blk_sum_parts(sums)),
        100_000_000,
        3_000_000,
    )
    sums, u = call(
        functools.partial(col_kernel, False),
        [S((64, 128), F32), S((2, 1024), F32)],
        [SMEM] * 3 + [VMEM] * 6,
        [pltpu.VMEM((2, 16, 1024), BF16)],
        (*meta, kt, *col_sum_parts(rows), mass_src),
        100_000_000,
        3_000_000,
    )
    mine, other = call(
        back_kernel,
        [S((32, 128, 256), BF16)] * 2,
        [SMEM] * 3 + [VMEM] * 3,
        [],
        (*meta, kt, u, raw),
        800_000_000,
        8_000_000,
    )
    came = swap(other)
    parts = blk_sum_parts(sums)
    tgt_own = reduce_targets(mine, came, core)
    *parts, v = call(
        toward_kernel,
        [S((2, 2, 128, 256), BF16)] * 4 + [S((2, 128), F32)],
        [SMEM] * 3 + [VMEM] * 8,
        [pltpu.VMEM((64, 128), F32), pltpu.VMEM((2, 256, 1024), F32)],
        (*meta, kt, u, tiles, *parts, mass_tgt),
        800_000_000,
        6_000_000,
    )
    src_own = reduce_sources(parts, even)
    src_aligned = (src_own / src_mass.astype(F32)[:, :, None]).astype(BF16)
    tgt_aligned = (tgt_own * v[:, :, None] / tgt_mass.astype(F32)[:, :, None]).astype(BF16)
    return (src_aligned, tgt_aligned)


def solution(mesh):
    in_specs = (
        P("blk", "col", None),
        P("blk", "col", None),
        P("blk", "col"),
        P("blk", "col"),
        P("blk", None),
        P("blk"),
        P(),
    )
    out_specs = (P("blk", "col", None), P("blk", "col", None))
    return jax.shard_map(program, mesh=mesh, in_specs=in_specs, out_specs=out_specs, check_vma=False)
```

```python
import functools
import math

import jax
import jax.numpy as jnp
from jax import lax
from jax.experimental import pallas as pl
from jax.experimental.pallas import tpu as pltpu
from jax.sharding import PartitionSpec as P


GROUPS = 7
TEMP = 0.02
OFFSET = 0.3
EPS = 1e-06
F32 = jnp.float32
BF16 = jnp.bfloat16
SMEM = pl.BlockSpec(memory_space=pltpu.SMEM)
VMEM = pl.BlockSpec(memory_space=pltpu.VMEM)
LIMIT = 16 * 1024 * 1024


def blk_perm(fn):
    pairs = []
    for i in range(32):
        y, x, k = fn(i // 8, (i // 2) % 4, i % 2)
        pairs.append((i, (y * 4 + x) * 2 + k))
    return pairs


def swap(v):
    return lax.ppermute(v, "blk", blk_perm(lambda y, x, k: (y, x, 1 - k)))


def over_x(v, d):
    return lax.ppermute(v, "blk", blk_perm(lambda y, x, k: (y, x ^ d, k)))


def over_y(v, d):
    return lax.ppermute(v, "blk", blk_perm(lambda y, x, k: (y ^ d, x, k)))


def over_first(v, d):
    return lax.ppermute(
        v, "blk", blk_perm(lambda y, x, k: (y, x ^ d, k) if k == 0 else (y ^ d, x, k))
    )


def over_second(v, d):
    return lax.ppermute(
        v, "blk", blk_perm(lambda y, x, k: (y ^ d, x, k) if k == 0 else (y, x ^ d, k))
    )


def over_z(v, d):
    return lax.ppermute(v, "col", [(i, i ^ d) for i in range(8)])


def along_z(v, odd):
    pairs = []
    for i in range(256):
        z, core = i % 8, (i // 8) % 2
        pairs.append((i, i - z + (((z + core + odd) ^ 1) - core - odd) % 8))
    return lax.ppermute(v, ("blk", "col"), pairs)


def pick(core, zero, one):
    return jnp.where(core == 0, zero, one)


def gather_targets(tgt_feat, core):
    came = swap(tgt_feat)
    pair = pick(core, jnp.stack([tgt_feat[0], came[0]]), jnp.stack([came[1], tgt_feat[1]]))
    near = [pair]
    for d in (1, 2, 3):
        near.append(over_first(pair, d))
    near = jnp.concatenate(near)
    parts = [near]
    for d in (1, 2, 3):
        parts.append(over_second(near, d))
    for n in range(4):
        parts.append(swap(parts[n]))
    return parts


def gather_sources(src_feat, even):
    came = along_z(src_feat, 0)
    pairs = [jnp.where(even, jnp.stack([src_feat, came]), jnp.stack([came, src_feat]))]
    for step in (2, 3, 4):
        pairs.append(along_z(pairs[-1], (step + 1) % 2))
    return pairs


def col_sum_parts(v):
    v = v + over_z(v.astype(BF16), 1).astype(F32)
    low = v.astype(BF16)
    return (v,) + tuple(over_z(low, d) for d in (5, 2, 6))


def blk_sum_parts(v):
    v = v + swap(v.astype(BF16)).astype(F32)
    low = v.astype(BF16)
    for d in (1, 3, 2):
        v = v + over_x(low, d).astype(F32)
    low = v.astype(BF16)
    parts = [v]
    for d in (1, 3, 2):
        parts.append(over_y(low, d))
    return parts


def reduce_targets(mine, came, core):
    q = (mine.astype(F32) + came.astype(F32)).astype(BF16).reshape(4, 8, 128, 256)
    s = q[0].astype(F32)
    for d in (1, 3, 2):
        s = s + over_first(q[d], d).astype(F32)
    s = s.astype(BF16).reshape(4, 2, 128, 256)
    t = s[0].astype(F32)
    for d in (1, 3, 2):
        came = over_second(s[d], d)
        t = t + came.astype(F32)
    keep = pick(core, t[0], t[1])
    came = swap(pick(core, t[1], t[0]).astype(BF16)).astype(F32)
    return pick(core, jnp.stack([keep, came]), jnp.stack([came, keep]))


def reduce_sources(parts, even):
    moving = along_z(parts[3], 1)
    for step in (2, 1):
        moving = along_z((parts[step].astype(F32) + moving.astype(F32)).astype(BF16), step % 2)
    pair = parts[0].astype(F32) + moving.astype(F32)
    came = along_z(jnp.where(even, pair[1], pair[0]).astype(BF16), 0)
    return jnp.where(even, pair[0], pair[1]) + came.astype(F32)


def group_of(meta, g):
    counts, candidates, home = meta
    first = lax.shift_right_logical(counts[0] + 1, 1)
    p = jnp.where(g >= first, 1, 0)
    k = jnp.minimum(2 * (g - first * p), 6)
    both = k + 1 < counts[p]
    return p, (home[candidates[p, k]], home[candidates[p, jnp.where(both, k + 1, k)]]), both


def live(meta):
    counts = meta[0]
    return lax.shift_right_logical(counts[0] + 1, 1) + lax.shift_right_logical(counts[1] + 1, 1)


def place():
    b = lax.axis_index("blk")
    return b, lax.axis_index("col"), b // 8, (b // 2) % 4, b % 2


def chunk_places(b, z):
    core = b % 2
    half = (z + core) & 7
    way = 1 - 2 * (half % 2)
    places = []
    for off in (0, -way, way, 2):
        first = 2 * (half // 2 + off)
        places.append([pl.multiple_of(((first + h - core) & 7) * 128, 128) for h in range(2)])
    return places


def unit(rows):
    x = rows.astype(F32)
    return (x * lax.rsqrt(jnp.mean(x * x, axis=-1, keepdims=True) + EPS)).astype(BF16)


def two_rows(v):
    high = v.astype(BF16).astype(F32)
    row = lax.broadcasted_iota(jnp.int32, (16, v.shape[1]), 0)
    return jnp.where(row == 0, high, jnp.where(row == 1, v - high, 0.0)).astype(BF16)


def unit_kernel(s0, s1, s2, s3, raw, unit_src):
    b, z = place()[:2]
    for ref, places in zip((s0, s1, s2, s3), chunk_places(b, z)):
        for h, at in enumerate(places):
            for p in range(2):
                chunk = ref[h, p]
                raw[p, pl.ds(at, 128), :] = chunk
                unit_src[p, pl.ds(at, 128), :] = unit(chunk)


def build_kernel(*refs):
    meta, refs = refs[:3], refs[3:]
    tgt = refs[:8]
    unit_src, mass, kt, tiles, rows, acc = refs[8:]
    n = live(meta)
    _, z, my_y, my_x, my_k = place()

    def fetch(g, targets):
        for h, j in enumerate(targets):
            i, owner = j % 2, j // 2
            dy, dx = (owner // 8) ^ my_y, ((owner // 2) % 4) ^ my_x
            first, second = jnp.where(i == 0, dx, dy), jnp.where(i == 0, dy, dx)
            at = first * 2 + owner % 2
            for near in (0, 1):

                @pl.when((i == my_k) == (near == 0))
                def _():
                    for a in range(4):

                        @pl.when(second == a)
                        def _():
                            tiles[g, h * 128 : (h + 1) * 128, :] = tgt[4 * near + a][at]

    acc[...] = jnp.zeros_like(acc)
    scale = math.log2(math.e) / (256 * TEMP)
    shift = OFFSET / TEMP * math.log2(math.e)

    def step(g, _):
        p, targets, both = group_of(meta, g)
        fetch(g, targets)
        tile = unit(tiles[g])
        keep = jnp.where(both, 1.0, 0.0)
        for c in range(4):
            cols = slice(c * 256, (c + 1) * 256)
            score = lax.dot_general(
                tile, unit_src[p, cols, :], (((1,), (1,)), ((), ())), preferred_element_type=F32
            )
            k = jnp.exp2(score * scale - shift)
            upper, lower = k[:128], k[128:] * keep
            kt[g, :128, cols] = upper.astype(BF16)
            kt[g, 128:, cols] = lower.astype(BF16)
            acc[p, :, cols] += (upper + lower).reshape(16, 8, 256).sum(axis=0)
        return 0

    lax.fori_loop(0, n, step, 0)

    def clear(g, _):
        kt[g] = jnp.zeros_like(kt[g])
        return 0

    lax.fori_loop(n, GROUPS, clear, 0)
    lane = lax.broadcasted_iota(jnp.int32, (1, 1024), 1) // 128
    for p in range(2):
        rows[p : p + 1, :] = jnp.sum(acc[p], axis=0, keepdims=True)
        own = jnp.concatenate([mass[p : p + 1, :].astype(F32)] * 8, axis=1)
        rows[2 + p : 3 + p, :] = jnp.where(lane == z, own, 0.0)


def col_kernel(first, *refs):
    meta, refs = refs[:3], refs[3:]
    if first:
        kt, r0, r1, r2, r3, tgt_mass, out, mass_out, u_rows = refs
        total = r0[...] + r1[...].astype(F32) + r2[...].astype(F32) + r3[...].astype(F32)
        mass = total[2:4]
        mass_out[...] = mass
    else:
        kt, r0, r1, r2, r3, mass_in, out, u_out, u_rows = refs
        total = r0[...] + r1[...].astype(F32) + r2[...].astype(F32) + r3[...].astype(F32)
        mass = mass_in[...]
    u = mass / total[0:2]
    if not first:
        u_out[...] = u
    for p in range(2):
        u_rows[p] = two_rows(u[p : p + 1])
    out[...] = jnp.zeros_like(out)

    found = []
    for g in range(GROUPS):
        p, targets, _ = group_of(meta, g)
        part = lax.dot_general(
            u_rows[p], kt[g], (((1,), (1,)), ((), ())), preferred_element_type=F32
        )
        found.append((targets, part[0:1] + part[1:2]))
    for targets, part in found:
        for h, j in enumerate(targets):
            out[pl.ds(j, 1), :] += part[:, h * 128 : (h + 1) * 128]
    if first:
        b = place()[0]
        out[pl.ds(64 + 2 * b, 1), :] = tgt_mass[0:1, :].astype(F32)
        out[pl.ds(65 + 2 * b, 1), :] = tgt_mass[1:2, :].astype(F32)


def row_kernel(*refs):
    meta, refs = refs[:3], refs[3:]
    kt, c0, c1, c2, c3, out, mass_out, v_all, acc = refs
    total = c0[...] + c1[...].astype(F32) + c2[...].astype(F32) + c3[...].astype(F32)
    mass_out[...] = total[64:]
    v_all[...] = total[64:] / total[:64]
    acc[...] = jnp.zeros_like(acc)

    found = []
    for g in range(GROUPS):
        p, targets, _ = group_of(meta, g)
        v = two_rows(jnp.concatenate([v_all[pl.ds(j, 1), :] for j in targets], axis=1))
        found.append((p, jnp.dot(v, kt[g], preferred_element_type=F32)[:8]))
    for p, part in found:
        acc[p] += part
    for p in range(2):
        out[p : p + 1, :] = acc[p, 0:1, :] + acc[p, 1:2, :]


def back_kernel(*refs):
    meta, refs = refs[:3], refs[3:]
    kt, u, raw, mine, other = refs
    _, _, my_y, my_x, my_k = place()
    mine[...] = jnp.zeros_like(mine)
    other[...] = jnp.zeros_like(other)

    def step(g, _):
        p, targets, _ = group_of(meta, g)
        row = jnp.where(p == 0, u[0:1, :], u[1:2, :])
        plan = (kt[g].astype(F32) * row).astype(BF16)
        both = jnp.dot(plan, raw[p], preferred_element_type=F32)
        for h, j in enumerate(targets):
            back = both[h * 128 : (h + 1) * 128]
            i, owner = j % 2, j // 2
            dy, dx = (owner // 8) ^ my_y, ((owner // 2) % 4) ^ my_x
            at = jnp.where(i == 0, dx * 8 + dy * 2, dy * 8 + dx * 2) + owner % 2

            @pl.when(i == my_k)
            def _():
                mine[at] = (mine[at].astype(F32) + back).astype(BF16)

            @pl.when(i != my_k)
            def _():
                other[at] = (other[at].astype(F32) + back).astype(BF16)

        return 0

    lax.fori_loop(0, live(meta), step, 0)


def toward_kernel(which, *refs):
    meta, refs = refs[:3], refs[3:]
    kt, u, tiles, c0, c1, c2, c3, mass = refs[:8]
    outs = refs[8 : 8 + len(which)]
    v_out, v_all, acc = refs[8 + len(which) :]
    total = c0[...] + c1[...].astype(F32) + c2[...].astype(F32) + c3[...].astype(F32)
    v_all[...] = mass[...] / total
    b, z = place()[:2]
    v_out[0:1, :] = v_all[pl.ds(2 * b, 1), :]
    v_out[1:2, :] = v_all[pl.ds(2 * b + 1, 1), :]
    places = chunk_places(b, z)
    acc[...] = jnp.zeros_like(acc)

    def step(g, _):
        p, targets, _ = group_of(meta, g)
        v = [jnp.broadcast_to(v_all[pl.ds(j, 1), :], (128, 128)).T for j in targets]
        v = jnp.concatenate(v, axis=0)
        tile = tiles[g].T
        for n, pair in enumerate(which):
            plan = []
            for at in places[pair]:
                row = jnp.where(p == 0, u[0:1, pl.ds(at, 128)], u[1:2, pl.ds(at, 128)])
                plan.append((kt[g, :, pl.ds(at, 128)].astype(F32) * row * v).astype(BF16))
            acc[p, n] += jnp.dot(tile, jnp.concatenate(plan, axis=1), preferred_element_type=F32)
        return 0

    lax.fori_loop(0, live(meta), step, 0)
    for n, ref in enumerate(outs):
        for h in range(2):
            for p in range(2):
                ref[h, p] = acc[p, n, :, h * 128 : (h + 1) * 128].astype(BF16).T


def call(kernel, out_shape, in_specs, scratch, args, flops, nbytes):
    return pl.pallas_call(
        kernel,
        out_shape=out_shape,
        in_specs=in_specs,
        out_specs=[VMEM] * len(out_shape),
        scratch_shapes=scratch,
        compiler_params=pltpu.CompilerParams(vmem_limit_bytes=LIMIT),
        cost_estimate=pl.CostEstimate(flops=flops, bytes_accessed=nbytes, transcendentals=0),
    )(*args)


def program(src_feat, tgt_feat, src_mass, tgt_mass, candidates, counts, tgt_home):
    core = lax.axis_index("blk") % 2
    meta = (counts, candidates, tgt_home)
    even = (lax.axis_index("col") + core) % 2 == 0
    sources = gather_sources(src_feat, even)
    targets = gather_targets(tgt_feat, core)
    S = jax.ShapeDtypeStruct
    raw, unit_src = call(
        unit_kernel, [S((2, 1024, 256), BF16)] * 2, [VMEM] * 4, [], sources, 2_000_000, 3_000_000
    )
    kt, tiles, rows = call(
        build_kernel,
        [S((GROUPS, 256, 1024), BF16), S((GROUPS, 256, 256), BF16), S((4, 1024), F32)],
        [SMEM] * 3 + [VMEM] * 10,
        [pltpu.VMEM((2, 8, 1024), F32)],
        (*meta, *targets, unit_src, src_mass),
        800_000_000,
        7_000_000,
    )
    sums, mass_src = call(
        functools.partial(col_kernel, True),
        [S((128, 128), F32), S((2, 1024), F32)],
        [SMEM] * 3 + [VMEM] * 6,
        [pltpu.VMEM((2, 16, 1024), BF16)],
        (*meta, kt, *col_sum_parts(rows), tgt_mass),
        100_000_000,
        3_000_000,
    )
    rows, mass_tgt = call(
        row_kernel,
        [S((2, 1024), F32), S((64, 128), F32)],
        [SMEM] * 3 + [VMEM] * 5,
        [pltpu.VMEM((64, 128), F32), pltpu.VMEM((2, 8, 1024), F32)],
        (*meta, kt, *blk_sum_parts(sums)),
        100_000_000,
        3_000_000,
    )
    sums, u = call(
        functools.partial(col_kernel, False),
        [S((64, 128), F32), S((2, 1024), F32)],
        [SMEM] * 3 + [VMEM] * 6,
        [pltpu.VMEM((2, 16, 1024), BF16)],
        (*meta, kt, *col_sum_parts(rows), mass_src),
        100_000_000,
        3_000_000,
    )
    mine, other = call(
        back_kernel,
        [S((32, 128, 256), BF16)] * 2,
        [SMEM] * 3 + [VMEM] * 3,
        [],
        (*meta, kt, u, raw),
        800_000_000,
        8_000_000,
    )
    came = swap(other)
    parts = blk_sum_parts(sums)
    tgt_own = reduce_targets(mine, came, core)
    rows = []
    for which in ((3,), (0, 1, 2)):
        *found, v = call(
            functools.partial(toward_kernel, which),
            [S((2, 2, 128, 256), BF16)] * len(which) + [S((2, 128), F32)],
            [SMEM] * 3 + [VMEM] * 8,
            [pltpu.VMEM((64, 128), F32), pltpu.VMEM((2, len(which), 256, 256), F32)],
            (*meta, kt, u, tiles, *parts, mass_tgt),
            200_000_000 * len(which),
            4_000_000,
        )
        rows = found + rows
    src_own = reduce_sources(rows, even)
    src_aligned = (src_own / src_mass.astype(F32)[:, :, None]).astype(BF16)
    tgt_aligned = (tgt_own * v[:, :, None] / tgt_mass.astype(F32)[:, :, None]).astype(BF16)
    return (src_aligned, tgt_aligned)


def solution(mesh):
    in_specs = (
        P("blk", "col", None),
        P("blk", "col", None),
        P("blk", "col"),
        P("blk", "col"),
        P("blk", None),
        P("blk"),
        P(),
    )
    out_specs = (P("blk", "col", None), P("blk", "col", None))
    return jax.shard_map(program, mesh=mesh, in_specs=in_specs, out_specs=out_specs, check_vma=False)
```
